256 devices in a mesh: dp: 8 (over z), space: 32 (over x, y, core).
Axes of the slice: x: 4, y: 4, z: 8, core: 2. Of those that a mesh axis runs over, the one named last changes fastest.
Arguments:
- lateral3: bfloat16 [32, 128, 128, 256], P('dp', 'space'), may hold values from -1200 to 1200
- lateral4: bfloat16 [32, 64, 64, 256], P('dp', 'space'), may hold values from -1200 to 1200
- lateral5: bfloat16 [32, 32, 32, 256], P('dp', 'space'), may hold values from -1200 to 1200
- conv_weight3: bfloat16 [3, 3, 256, 256], P(None, None, None, ('dp', 'space')), may hold values from -0.125 to 0.125
- conv_weight4: bfloat16 [3, 3, 256, 256], P(None, None, None, ('dp', 'space')), may hold values from -0.125 to 0.125
- conv_weight5: bfloat16 [3, 3, 256, 256], P(None, None, None, ('dp', 'space')), may hold values from -0.125 to 0.125
- norm_gain3: float32 [256], replicated, may hold values from 0.1 to 1.9
- norm_shift3: float32 [256], replicated, may hold values from -3 to 3
- norm_gain4: float32 [256], replicated, may hold values from 0.1 to 1.9
- norm_shift4: float32 [256], replicated, may hold values from -3 to 3
- norm_gain5: float32 [256], replicated, may hold values from 0.1 to 1.9
- norm_shift5: float32 [256], replicated, may hold values from -3 to 3
Outputs:
- pyramid3: float32 [32, 128, 128, 256], P('dp', 'space')
- pyramid4: float32 [32, 64, 64, 256], P('dp', 'space')
- pyramid5: float32 [32, 32, 32, 256], P('dp', 'space')
The draws below stay inside these ranges and needn't reach their ends.
All inputs are finite; a program needn't handle non-finite values.
Results may differ from the reference program's by a relative error of at most 0.007.
Values may be sent and summed in bfloat16 or wider, within the bound.
A program may use at most 64 MiB of HBM per device.

```python
import jax
import jax.numpy as jnp
from jax import lax

C = 256
G = 32
W3 = 128
H5 = 32
H4 = 64
H3 = 128
W4 = 64
W5 = 32
BATCH = 32


def lateral_field(key, image_count, row_count, column_count, channel_count):
    pattern_key, column_key = jax.random.split(key, 2)
    heights = jnp.arange(row_count, dtype=jnp.float32) / max(row_count - 1, 1)
    shape_full = (image_count, row_count, column_count, channel_count)
    pattern = jnp.clip(jax.random.normal(pattern_key, shape_full, jnp.float32), -6.0, 6.0)
    row_scale = 10.0 ** heights
    column_scale = 10.0 ** jax.random.uniform(column_key, (image_count, 1, column_count, 1), jnp.float32, 0.0, 1.0)
    return pattern * row_scale[None, :, None, None] * column_scale


def draw_lateral3(key, part):
    return lateral_field(jax.random.fold_in(key, 3), BATCH, H3, W3, C).astype(jnp.bfloat16)


def draw_lateral4(key, part):
    return lateral_field(jax.random.fold_in(key, 4), BATCH, H4, W4, C).astype(jnp.bfloat16)


def draw_lateral5(key, part):
    return lateral_field(jax.random.fold_in(key, 5), BATCH, H5, W5, C).astype(jnp.bfloat16)


def steps_of(rng, dims, shards, least, largest):
    loudness, own = 1.0, jax.random.fold_in(rng, 6)
    for dim, parts in shards:
        steps = jnp.exp(jax.random.uniform(jax.random.fold_in(own, dim), (parts,), jnp.float32, least / len(shards), largest / len(shards)))
        loudness = loudness * jnp.repeat(steps, dims[dim] // parts).reshape([-1 if axis == dim else 1 for axis in range(len(dims))])
    return loudness


def scatter_about(rng, extent, scale, reach, pieces=(), kind=jnp.bfloat16):
    entries = jax.random.normal(rng, extent, jnp.float32) * scale
    if len(pieces) > 0:
        entries = steps_of(rng, extent, pieces, -0.22, 0.18) * entries
    return jnp.clip(entries, min=-reach, max=reach).astype(kind)


def setup_inputs(seed: int = 0) -> dict:
    streams_of = jax.random.split(jax.random.key(seed), 13)
    lateral3 = draw_lateral3(jax.random.fold_in(streams_of[12], 71), 0)
    lateral4 = draw_lateral4(jax.random.fold_in(streams_of[12], 71), 0)
    lateral5 = draw_lateral5(jax.random.fold_in(streams_of[12], 71), 0)
    conv_weight3 = scatter_about(streams_of[3], (3, 3, C, C), (9 * C) ** -0.5, 0.125, ((3, 256),))
    conv_weight4 = scatter_about(streams_of[4], (3, 3, C, C), (9 * C) ** -0.5, 0.125, ((3, 256),))
    conv_weight5 = scatter_about(streams_of[5], (3, 3, C, C), (9 * C) ** -0.5, 0.125, ((3, 256),))
    norm_gain3 = jnp.clip(1.0 + 0.18 * jax.random.normal(streams_of[6], (C,), jnp.float32), 0.1, 1.9)
    norm_shift3 = scatter_about(streams_of[7], (C,), 0.5, 3.0, (), jnp.float32)
    norm_gain4 = jnp.clip(1.0 + 0.18 * jax.random.normal(streams_of[8], (C,), jnp.float32), 0.1, 1.9)
    norm_shift4 = scatter_about(streams_of[9], (C,), 0.5, 3.0, (), jnp.float32)
    norm_gain5 = jnp.clip(1.0 + 0.18 * jax.random.normal(streams_of[10], (C,), jnp.float32), 0.1, 1.9)
    norm_shift5 = scatter_about(streams_of[11], (C,), 0.5, 3.0, (), jnp.float32)
    return {"lateral3": lateral3, "lateral4": lateral4, "lateral5": lateral5, "conv_weight3": conv_weight3, "conv_weight4": conv_weight4, "conv_weight5": conv_weight5, "norm_gain3": norm_gain3, "norm_shift3": norm_shift3, "norm_gain4": norm_gain4, "norm_shift4": norm_shift4, "norm_gain5": norm_gain5, "norm_shift5": norm_shift5}


epsilon = 1e-05

def enlarge(values):
    return jnp.repeat(jnp.repeat(values, 2, axis=0), 2, axis=1)

def convolve(single, kernel):
    result = lax.conv_general_dilated(single[None], kernel, (1, 1), ((1, 1), (1, 1)), dimension_numbers=('NHWC', 'HWIO', 'NHWC'), preferred_element_type=jnp.float32)
    return result[0]

def group_norm(values, gain_vector, shift_vector):
    blocks = values.reshape(values.shape[0], values.shape[1], G, values.shape[2] // G)
    center = lax.optimization_barrier(jnp.mean(blocks, axis=(0, 1, 3), keepdims=True))
    deviation = blocks - center
    spread = lax.optimization_barrier(jnp.mean(deviation * deviation, axis=(0, 1, 3), keepdims=True))
    scaled = deviation * lax.rsqrt(spread + epsilon)
    return scaled.reshape(values.shape) * gain_vector + shift_vector

def reference(lateral3, lateral4, lateral5, conv_weight3, conv_weight4, conv_weight5, norm_gain3, norm_shift3, norm_gain4, norm_shift4, norm_gain5, norm_shift5):

    def single_image(triple):
        fine_in, middle_in, coarse_in = triple
        merged5 = coarse_in
        merged4 = (middle_in.astype(jnp.float32) + enlarge(merged5).astype(jnp.float32)).astype(jnp.bfloat16)
        merged3 = (fine_in.astype(jnp.float32) + enlarge(merged4).astype(jnp.float32)).astype(jnp.bfloat16)
        output3 = group_norm(convolve(merged3, conv_weight3), norm_gain3, norm_shift3)
        output4 = group_norm(convolve(merged4, conv_weight4), norm_gain4, norm_shift4)
        output5 = group_norm(convolve(merged5, conv_weight5), norm_gain5, norm_shift5)
        return (output3, output4, output5)
    pyramid3, pyramid4, pyramid5 = lax.map(single_image, (lateral3, lateral4, lateral5))
    return (pyramid3, pyramid4, pyramid5)
```

```python
import jax
import jax.numpy as jnp
from jax import lax
from jax.experimental import pallas as pl
from jax.experimental.pallas import tpu as pltpu
from jax.sharding import Mesh
from jax.sharding import PartitionSpec as P

SPACE = ("x", "y", "c")
AXES = ("z", "x", "y", "c")
MESH = pl.DeviceIdType.MESH
NZ, NX, NY, NC = 8, 4, 4, 2
STRIPS = NX * NY * NC
C, G, B = 256, 32, 4
HALF = 128
LEVELS = ((4, 128), (2, 64), (1, 32))
epsilon = 1e-05
F32, BF16 = jnp.float32, jnp.bfloat16


def wrap(value, size):
    return lax.rem(value + 2 * size, size)


def put(ref, image, row, value):
    n = value.shape[0]
    rounded = value.astype(BF16)
    wide = rounded.astype(F32)
    place = lax.broadcasted_iota(jnp.int32, wide.shape, 0)
    ref[1, image, row] = rounded
    ref[0, image, row] = jnp.where(place == 0, 0.0, pltpu.roll(wide, 1, 0)).astype(BF16)
    ref[2, image, row] = jnp.where(place == n - 1, 0.0, pltpu.roll(wide, n - 1, 0)).astype(BF16)


def repeat_matrix(n):
    rows = lax.broadcasted_iota(jnp.int32, (2 * n, n), 0)
    columns = lax.broadcasted_iota(jnp.int32, (2 * n, n), 1)
    return (lax.shift_right_logical(rows, 1) == columns).astype(F32).astype(BF16)


def kernel(
    lat3, lat4, lat5, w3, w4, w5,
    f3, f4, f5, center_ref, scale_ref,
    w_all, w_tap, raw, l3, l4, l5, h3, h4, h5, x3, x4, x5, sums, stat_a, stat_b,
    local_sem, raw_send, raw_recv, z_send, z_recv, x_send, x_recv, c_send, c_recv,
    halo_send, halo_recv, stat_send, stat_recv,
):
    z, x, y, c = (lax.axis_index(a) for a in AXES)
    slot = y * 2 + c
    other = 1 - c
    strip = (x * NY + y) * 2 + c
    nxt, prv = wrap(strip + 1, STRIPS), wrap(strip - 1, STRIPS)
    next_id = (z, nxt // 8, lax.rem(nxt // 2, 4), lax.rem(nxt, 2))
    prev_id = (z, prv // 8, lax.rem(prv // 2, 4), lax.rem(prv, 2))
    partner = (z, x, y, other)

    ring_ids = [(z, x, wrap(y + dy, NY), k) for dy in (1, 2, 3) for k in range(2)] + [partner]
    x_ids = [(z, wrap(x + d, NX), y, c) for d in (1, 2, 3)]
    z_ids = [(wrap(z + d, NZ), x, y, c) for d in range(1, NZ)]

    barrier = pltpu.get_barrier_semaphore()
    greeted = z_ids + x_ids + ring_ids + [next_id, prev_id]
    for who in greeted:
        pl.semaphore_signal(barrier, 1, device_id=who, device_id_type=MESH)

    loads = [
        pltpu.make_async_copy(lat5, l5, local_sem.at[0]),
        pltpu.make_async_copy(lat4, l4, local_sem.at[1]),
        pltpu.make_async_copy(lat3, l3, local_sem.at[2]),
    ]
    for copy in loads:
        copy.start()

    first = strip == 0
    last = strip == STRIPS - 1
    up5, up4 = repeat_matrix(32), repeat_matrix(64)

    def rows5(image, row, source, hidden=None):
        value = source.astype(F32)
        if hidden is not None:
            value = jnp.where(hidden, 0.0, value)
        put(x5, image, row, value)

    def rows4(image, row, source, coarse, hidden=None):
        value = source.astype(F32) + jnp.dot(up5, coarse, preferred_element_type=F32)
        if hidden is not None:
            value = jnp.where(hidden, 0.0, value)
        put(x4, image, row, value)

    def rows3(image, row, source, hidden=None):
        middle = x4[1, image, (row + 1) // 2]
        value = source.astype(F32) + jnp.dot(up4, middle, preferred_element_type=F32)
        if hidden is not None:
            value = jnp.where(hidden, 0.0, value)
        put(x3, image, row, value)

    loads[0].wait()
    loads[1].wait()

    def own_coarse(image, _):
        rows5(image, 1, l5[image, 0])
        for q in (1, 2):
            rows4(image, q, l4[image, q - 1], l5[image, 0])
        return 0

    lax.fori_loop(0, B, own_coarse, 0)

    pl.semaphore_wait(barrier, len(greeted))

    weights = (w3, w4, w5)
    raw_copies = []
    mine = pl.ds(pl.multiple_of(c * HALF, HALF), HALF)
    theirs = pl.ds(pl.multiple_of(other * HALF, HALF), HALF)
    for level in range(3):
        keep = pltpu.make_async_copy(
            weights[level].at[:, :, mine], raw.at[slot, level], local_sem.at[3 + level]
        )
        keep.start()
        raw_copies.append(keep)
    raw_remote = []
    for level in range(3):
        for dy in (1, 2, 3):
            for k in range(2):
                raw_remote.append(
                    pltpu.make_async_remote_copy(
                        weights[level].at[:, :, k * HALF : (k + 1) * HALF],
                        raw.at[slot, level],
                        raw_send.at[level, (dy - 1) * 2 + k],
                        raw_recv.at[level, (dy - 1) * 2 + c],
                        device_id=(z, x, wrap(y + dy, NY), k),
                        device_id_type=MESH,
                    )
                )
        raw_remote.append(
            pltpu.make_async_remote_copy(
                weights[level].at[:, :, theirs],
                raw.at[slot, level],
                raw_send.at[level, 6],
                raw_recv.at[level, 6],
                device_id=partner,
                device_id_type=MESH,
            )
        )
    for copy in raw_remote:
        copy.start()

    halo = []
    for number, (source, target, who) in enumerate((
        (lat5.at[:, 0], h5.at[0], next_id),
        (lat5.at[:, 0], h5.at[1], prev_id),
        (lat4.at[:, 1], h4.at[0], next_id),
        (lat4.at[:, 0], h4.at[1], prev_id),
        (lat3.at[:, 3], h3.at[0], next_id),
        (lat3.at[:, 0], h3.at[1], prev_id),
    )):
        copy = pltpu.make_async_remote_copy(
            source, target, halo_send.at[number], halo_recv.at[number],
            device_id=who, device_id_type=MESH,
        )
        copy.start()
        halo.append(copy)

    loads[2].wait()

    def own_fine(image, _):
        for r in (1, 2, 3, 4):
            rows3(image, r, l3[image, r - 1])
        return 0

    lax.fori_loop(0, B, own_fine, 0)

    z_copies, x_copies, c_copies = {}, {}, {}
    for level in range(3):
        raw_copies[level].wait()
        for i in range(7):
            pltpu.make_async_remote_copy(
                raw.at[0, level], raw.at[0, level],
                raw_send.at[level, i], raw_recv.at[level, i],
                device_id=partner, device_id_type=MESH,
            ).wait_recv()
        for kh in range(3):
            rows = [raw[s, level, kh].astype(F32) for s in range(8)]
            for kw in range(3):
                tile = jnp.concatenate([r[kw : kw + 1] for r in rows], axis=0)
                w_all[c, level, x, z, kh * 3 + kw] = tile.astype(BF16)
        for d in range(1, NZ):
            copy = pltpu.make_async_remote_copy(
                w_all.at[c, level, x, z], w_all.at[c, level, x, z],
                z_send.at[level, d - 1], z_recv.at[level, d - 1],
                device_id=z_ids[d - 1], device_id_type=MESH,
            )
            z_copies[level, d] = copy
    for level in range(3):
        for d in (4, 3, 5, 2, 6, 1, 7):
            z_copies[level, d].start()

    for copy in halo:
        copy.wait_recv()

    def outer(image, _):
        rows5(image, 0, h5[0, image], first)
        rows5(image, 2, h5[1, image], last)
        rows4(image, 0, h4[0, image], h5[0, image], first)
        rows4(image, 3, h4[1, image], h5[1, image], last)
        rows3(image, 0, h3[0, image], first)
        rows3(image, 5, h3[1, image], last)
        return 0

    lax.fori_loop(0, B, outer, 0)

    def piece_to_partner(level, d):
        where = wrap(x - d, NX)
        copy = pltpu.make_async_remote_copy(
            w_all.at[c, level, where], w_all.at[c, level, where],
            c_send.at[level, d], c_recv.at[level, d],
            device_id=partner, device_id_type=MESH,
        )
        copy.start()
        c_copies[level, d] = copy

    for level in range(3):
        for d in range(1, NZ):
            z_copies[level, d].wait_recv()
        for d in (2, 1, 3):
            copy = pltpu.make_async_remote_copy(
                w_all.at[c, level, x], w_all.at[c, level, x],
                x_send.at[level, d - 1], x_recv.at[level, d - 1],
                device_id=x_ids[d - 1], device_id_type=MESH,
            )
            copy.start()
            x_copies[level, d] = copy
        piece_to_partner(level, 0)

    def receive_x(level):
        for d in (1, 3, 2):
            x_copies[level, d].wait_recv()
            piece_to_partner(level, d)

    def receive_partner(level):
        for d in range(NX):
            c_copies[level, d].wait_recv()

    def ready(level):
        def tap(t, _):
            for half in range(2):
                for o in range(0, 32, 2):
                    pair = [
                        w_all[half, level, (o + k) % 4, (o + k) // 4, t].astype(F32) for k in range(2)
                    ]
                    w_tap[t, o * 8 : o * 8 + 16, half * HALF : (half + 1) * HALF] = jnp.concatenate(
                        pair, axis=0
                    ).astype(BF16)
            return 0

        lax.fori_loop(0, 9, tap, 0)

    def product(left, t):
        return lax.dot_general(
            left, w_tap[t], (((1,), (1,)), ((), ())), preferred_element_type=F32
        )

    def conv3(image, _):
        total = None
        for t in range(9):
            kh, kw = t // 3, t % 3
            left = x3[kw, image, kh : kh + 4].reshape(4 * 128, C)
            part = product(left, t)
            total = part if total is None else total + part
        f3[image] = total.reshape(4, 128, C)
        sums[0, pl.ds(image, 1)] = jnp.sum(total, axis=0, keepdims=True)
        sums[1, pl.ds(image, 1)] = jnp.sum(total * total, axis=0, keepdims=True)
        return 0

    def conv_small(level, source, target):
        rows, width = LEVELS[level]
        total = None
        for t in range(9):
            kh, kw = t // 3, t % 3
            left = source[kw, :, kh : kh + rows].reshape(B * rows * width, C)
            part = product(left, t)
            total = part if total is None else total + part
        target[...] = total.reshape(B, rows, width, C)
        for image in range(B):
            one = total[image * rows * width : (image + 1) * rows * width]
            sums[2 * level, image : image + 1] = jnp.sum(one, axis=0, keepdims=True)
            sums[2 * level + 1, image : image + 1] = jnp.sum(one * one, axis=0, keepdims=True)

    receive_x(0)
    receive_partner(0)
    ready(0)
    lax.fori_loop(0, 2, conv3, 0)
    receive_x(1)
    lax.fori_loop(2, B, conv3, 0)
    receive_partner(1)
    ready(1)
    conv_small(1, x4, f4)
    receive_x(2)
    receive_partner(2)
    ready(2)
    conv_small(2, x5, f5)

    channel = lax.broadcasted_iota(jnp.int32, (C, 128), 0)
    lane = lax.broadcasted_iota(jnp.int32, (C, 128), 1)
    member = lax.shift_right_logical(channel, 3)

    def selector(image):
        return (lane == member + 32 * image).astype(F32)

    packed = jnp.zeros((8, 128), F32)
    for image in range(B):
        packed += lax.dot_general(
            sums[:, image], selector(image), (((1,), (0,)), ((), ())),
            precision=lax.Precision.HIGHEST, preferred_element_type=F32,
        )
    stat_a[slot] = packed
    stats = []
    for i, (dy, k) in enumerate([(dy, k) for dy in (1, 2, 3) for k in range(2)] + [(0, None)]):
        copy = pltpu.make_async_remote_copy(
            stat_a.at[slot], stat_a.at[slot],
            stat_send.at[i], stat_recv.at[6 if k is None else (dy - 1) * 2 + c],
            device_id=ring_ids[i], device_id_type=MESH,
        )
        copy.start()
        stats.append(copy)
    for i in range(7):
        pltpu.make_async_remote_copy(
            stat_a.at[0], stat_a.at[0], stat_send.at[i], stat_recv.at[i],
            device_id=partner, device_id_type=MESH,
        ).wait_recv()
    stat_b[x] = jnp.sum(stat_a[...], axis=0)
    for d in (1, 2, 3):
        copy = pltpu.make_async_remote_copy(
            stat_b.at[x], stat_b.at[x], stat_send.at[6 + d], stat_recv.at[6 + d],
            device_id=x_ids[d - 1], device_id_type=MESH,
        )
        copy.start()
        stats.append(copy)
    for copy in stats[7:]:
        copy.wait_recv()
    whole = jnp.sum(stat_b[...], axis=0)

    spreads = []
    for level, (rows, width) in enumerate(LEVELS):
        volume = float(rows * STRIPS * width * (C // G))
        mean = whole[2 * level : 2 * level + 1] / volume
        square = whole[2 * level + 1 : 2 * level + 2] / volume
        spread = jnp.maximum(square - mean * mean, 0.0)
        spreads += [mean, lax.rsqrt(spread + epsilon)]
    spreads += [jnp.zeros((2, 128), F32)]
    table = jnp.concatenate(spreads, axis=0)
    for image in range(B):
        spread_out = lax.dot_general(
            table, selector(image), (((1,), (1,)), ((), ())),
            precision=lax.Precision.HIGHEST, preferred_element_type=F32,
        )
        for level in range(3):
            center_ref[level, image : image + 1] = spread_out[2 * level : 2 * level + 1]
            scale_ref[level, image : image + 1] = spread_out[2 * level + 1 : 2 * level + 2]

    for group in (raw_remote, halo, z_copies.values(), x_copies.values(), c_copies.values(), stats):
        for copy in group:
            copy.wait_send()


def local(
    lateral3, lateral4, lateral5, conv_weight3, conv_weight4, conv_weight5,
    norm_gain3, norm_shift3, norm_gain4, norm_shift4, norm_gain5, norm_shift5,
):
    dma = pltpu.SemaphoreType.DMA
    vmem = pl.BlockSpec(memory_space=pltpu.VMEM)
    anywhere = pl.BlockSpec(memory_space=pl.ANY)
    f3, f4, f5, center, scale = pl.pallas_call(
        kernel,
        out_shape=[jax.ShapeDtypeStruct((B, r, w, C), F32) for r, w in LEVELS]
        + [jax.ShapeDtypeStruct((3, B, C), F32)] * 2,
        in_specs=[anywhere] * 3 + [vmem] * 3,
        out_specs=[vmem] * 5,
        scratch_shapes=[
            pltpu.VMEM((2, 3, NX, NZ, 9, 8, HALF), BF16),
            pltpu.VMEM((9, C, C), BF16),
            pltpu.VMEM((8, 3, 3, 3, HALF), BF16),
            pltpu.VMEM((B, 4, 128, C), BF16),
            pltpu.VMEM((B, 2, 64, C), BF16),
            pltpu.VMEM((B, 1, 32, C), BF16),
            pltpu.VMEM((2, B, 128, C), BF16),
            pltpu.VMEM((2, B, 64, C), BF16),
            pltpu.VMEM((2, B, 32, C), BF16),
            pltpu.VMEM((3, B, 6, 128, C), BF16),
            pltpu.VMEM((3, B, 4, 64, C), BF16),
            pltpu.VMEM((3, B, 3, 32, C), BF16),
            pltpu.VMEM((8, B, C), F32),
            pltpu.VMEM((8, 8, 128), F32),
            pltpu.VMEM((NX, 8, 128), F32),
            dma((6,)),
            dma((3, 7)), dma((3, 7)),
            dma((3, 7)), dma((3, 7)),
            dma((3, 3)), dma((3, 3)),
            dma((3, 4)), dma((3, 4)),
            dma((6,)), dma((6,)),
            dma((10,)), dma((10,)),
        ],
        compiler_params=pltpu.CompilerParams(
            collective_id=0, has_side_effects=True, vmem_limit_bytes=48 * 2**20
        ),
        name="neck",
    )(
        lateral3, lateral4, lateral5,
        conv_weight3.reshape(3, 3, C), conv_weight4.reshape(3, 3, C), conv_weight5.reshape(3, 3, C),
    )

    def normalize(values, level, gain, shift):
        deviation = values - center[level][:, None, None, :]
        return deviation * scale[level][:, None, None, :] * gain + shift

    return (
        normalize(f3, 0, norm_gain3, norm_shift3),
        normalize(f4, 1, norm_gain4, norm_shift4),
        normalize(f5, 2, norm_gain5, norm_shift5),
    )


def solution(mesh):
    torus = Mesh(mesh.devices.reshape(NZ, NX, NY, NC), AXES)
    strips = P("z", SPACE, None, None)
    kernels = P(None, None, None, AXES)
    return jax.shard_map(
        local,
        mesh=torus,
        in_specs=(strips,) * 3 + (kernels,) * 3 + (P(),) * 6,
        out_specs=(strips,) * 3,
        check_vma=False,
    )
```

```python
import jax
import jax.numpy as jnp
from jax import lax
from jax.experimental import pallas as pl
from jax.experimental.pallas import tpu as pltpu
from jax.sharding import Mesh
from jax.sharding import PartitionSpec as P

SPACE = ("x", "y", "c")
AXES = ("z", "x", "y", "c")
MESH = pl.DeviceIdType.MESH
NZ, NX, NY, NC = 8, 4, 4, 2
STRIPS = NX * NY * NC
C, G, B = 256, 32, 4
HALF = 128
LEVELS = ((4, 128), (2, 64), (1, 32))
epsilon = 1e-05
F32, BF16 = jnp.float32, jnp.bfloat16


def wrap(value, size):
    return lax.rem(value + 2 * size, size)


def put(ref, image, row, value):
    n = value.shape[0]
    rounded = value.astype(BF16)
    wide = rounded.astype(F32)
    place = lax.broadcasted_iota(jnp.int32, wide.shape, 0)
    ref[1, image, row] = rounded
    ref[0, image, row] = jnp.where(place == 0, 0.0, pltpu.roll(wide, 1, 0)).astype(BF16)
    ref[2, image, row] = jnp.where(place == n - 1, 0.0, pltpu.roll(wide, n - 1, 0)).astype(BF16)


def repeat_matrix(n):
    rows = lax.broadcasted_iota(jnp.int32, (2 * n, n), 0)
    columns = lax.broadcasted_iota(jnp.int32, (2 * n, n), 1)
    return (lax.shift_right_logical(rows, 1) == columns).astype(F32).astype(BF16)


def kernel(
    lat3, lat4, lat5, w3, w4, w5, g3, b3, g4, b4, g5, b5,
    f3, f4, f5, table_ref,
    w_all, w_tap, raw, l3, l4, l5, h3, h4, h5, x3, x4, x5, sums, stat_a, stat_b, params,
    local_sem, raw_send, raw_recv, z_send, z_recv, x_send, x_recv, y_send, y_recv, c_send, c_recv,
    halo_send, halo_recv, stat_send, stat_recv,
):
    z, x, y, c = (lax.axis_index(a) for a in AXES)
    slot = y * 2 + c
    other = 1 - c
    strip = (x * NY + y) * 2 + c
    nxt, prv = wrap(strip + 1, STRIPS), wrap(strip - 1, STRIPS)
    next_id = (z, nxt // 8, lax.rem(nxt // 2, 4), lax.rem(nxt, 2))
    prev_id = (z, prv // 8, lax.rem(prv // 2, 4), lax.rem(prv, 2))
    partner = (z, x, y, other)

    ring_ids = [(z, x, wrap(y + dy, NY), k) for dy in (1, 2, 3) for k in range(2)] + [partner]
    y_ids = [(z, x, wrap(y + d, NY), c) for d in (1, 2, 3)]
    x_ids = [(z, wrap(x + d, NX), y, c) for d in (1, 2, 3)]
    z_ids = [(wrap(z + d, NZ), x, y, c) for d in range(1, NZ)]

    barrier = pltpu.get_barrier_semaphore()
    greeted = z_ids + x_ids + ring_ids + [next_id, prev_id]
    for who in greeted:
        pl.semaphore_signal(barrier, 1, device_id=who, device_id_type=MESH)

    loads = [
        pltpu.make_async_copy(lat5, l5, local_sem.at[0]),
        pltpu.make_async_copy(lat4, l4, local_sem.at[1]),
        pltpu.make_async_copy(lat3, l3, local_sem.at[2]),
    ]
    for copy in loads:
        copy.start()
    weights = (w3, w4, w5)
    mine = pl.ds(pl.multiple_of(c * HALF, HALF), HALF)
    theirs = pl.ds(pl.multiple_of(other * HALF, HALF), HALF)
    for level in range(3):
        pltpu.make_async_copy(
            weights[level].at[:, :, mine], raw.at[slot, level], local_sem.at[3]
        ).start()
    for i, source in enumerate((g3, b3, g4, b4, g5, b5)):
        pltpu.make_async_copy(source, params.at[i], local_sem.at[4]).start()

    def remote(source, target, sends, recvs, who):
        pltpu.make_async_remote_copy(
            source, target, sends, recvs, device_id=who, device_id_type=MESH
        ).start()

    def all_of(total, sends, recvs):
        return pltpu.make_async_remote_copy(
            total, total, sends, recvs, device_id=partner, device_id_type=MESH
        )

    with jax.named_scope("s3_barrier"):
        pl.semaphore_wait(barrier, len(greeted))

    for level in range(3):
        for dy in (2, 1, 3):
            for k in range(2):
                remote(
                    weights[level].at[:, :, k * HALF : (k + 1) * HALF], raw.at[slot, level],
                    raw_send.at[0], raw_recv.at[level], (z, x, wrap(y + dy, NY), k),
                )
        remote(
            weights[level].at[:, :, theirs], raw.at[slot, level],
            raw_send.at[0], raw_recv.at[level], partner,
        )

    for level, lateral, held, lowest in ((2, lat5, h5, 0), (1, lat4, h4, 1), (0, lat3, h3, 3)):
        remote(lateral.at[:, lowest], held.at[0], halo_send.at[level], halo_recv.at[level], next_id)
        remote(lateral.at[:, 0], held.at[1], halo_send.at[level], halo_recv.at[level], prev_id)

    first = strip == 0
    last = strip == STRIPS - 1
    up5, up4 = repeat_matrix(32), repeat_matrix(64)

    def rows5(image, row, source, hidden=None):
        value = source.astype(F32)
        if hidden is not None:
            value = jnp.where(hidden, 0.0, value)
        put(x5, image, row, value)

    def rows4(image, row, source, coarse, hidden=None):
        value = source.astype(F32) + jnp.dot(up5, coarse, preferred_element_type=F32)
        if hidden is not None:
            value = jnp.where(hidden, 0.0, value)
        put(x4, image, row, value)

    def rows3(image, row, source, hidden=None):
        middle = x4[1, image, (row + 1) // 2]
        value = source.astype(F32) + jnp.dot(up4, middle, preferred_element_type=F32)
        if hidden is not None:
            value = jnp.where(hidden, 0.0, value)
        put(x3, image, row, value)

    for copy in loads:
        copy.wait()

    def own(image, _):
        rows5(image, 1, l5[image, 0])
        for q in (1, 2):
            rows4(image, q, l4[image, q - 1], l5[image, 0])
        for r in (1, 2, 3, 4):
            rows3(image, r, l3[image, r - 1])
        return 0

    with jax.named_scope("s5_own"):
        lax.fori_loop(0, B, own, 0)

    DIRECT, SPLIT = slice(0, 4), slice(4, 9)
    quarter = pl.ds(2 * y, 2)
    pltpu.make_async_copy(raw.at[0], raw.at[0], local_sem.at[3]).wait()

    for level in range(3):
        with jax.named_scope(f"s6_raw{level}"):
            all_of(raw.at[0:7, level], raw_send.at[0], raw_recv.at[level]).wait_recv()
        for kh in range(3):
            rows = [raw[s, level, kh].astype(F32) for s in range(8)]
            for kw in range(3):
                tile = jnp.concatenate([r[kw : kw + 1] for r in rows], axis=0)
                w_all[c, level, x, z, kh * 3 + kw] = tile.astype(BF16)
        for part, taps in ((1, SPLIT), (0, DIRECT)):
            for d in (4, 3, 5, 2, 6, 1, 7):
                ref = w_all.at[c, level, x, z, taps]
                remote(ref, ref, z_send.at[0], z_recv.at[level, part], z_ids[d - 1])

    def outer(image, _):
        rows5(image, 0, h5[0, image], first)
        rows5(image, 2, h5[1, image], last)
        rows4(image, 0, h4[0, image], h5[0, image], first)
        rows4(image, 3, h4[1, image], h5[1, image], last)
        rows3(image, 0, h3[0, image], first)
        rows3(image, 5, h3[1, image], last)
        return 0

    def to_partner(level, part, ref):
        remote(ref, ref, c_send.at[0], c_recv.at[level, part], partner)

    def after_z(level, part):
        taps = SPLIT if part else DIRECT
        with jax.named_scope(f"z{level}{part}"):
            all_of(w_all.at[c, level, x, 0:7, taps], z_send.at[0], z_recv.at[level, part]).wait_recv()
        ref = w_all.at[c, level, x, quarter, taps] if part else w_all.at[c, level, x, :, taps]
        for d in (2, 1, 3):
            remote(ref, ref, x_send.at[part], x_recv.at[level, part], x_ids[d - 1])
        to_partner(level, part, w_all.at[c, level, x, :, taps])

    def after_x(level, part):
        with jax.named_scope(f"x{level}{part}"):
            if part:
                total = w_all.at[c, level, 0:3, 0:2, SPLIT]
            else:
                total = w_all.at[c, level, 0:3, :, DIRECT]
            all_of(total, x_send.at[part], x_recv.at[level, part]).wait_recv()
        for d in (1, 3, 2):
            where = wrap(x - d, NX)
            if part:
                ref = w_all.at[c, level, where, quarter, SPLIT]
                for e in (2, 1, 3):
                    remote(ref, ref, y_send.at[0], y_recv.at[level], y_ids[e - 1])
            else:
                to_partner(level, part, w_all.at[c, level, where, :, DIRECT])

    def after_y(level):
        with jax.named_scope(f"y{level}"):
            all_of(w_all.at[c, level, 0:3, 0:6, SPLIT], y_send.at[0], y_recv.at[level]).wait_recv()
        for d in (1, 2, 3):
            to_partner(level, 1, w_all.at[c, level, wrap(x - d, NX), :, SPLIT])

    def receive_partner(level, part):
        taps = SPLIT if part else DIRECT
        with jax.named_scope(f"c{level}{part}"):
            all_of(w_all.at[other, level, :, :, taps], c_send.at[0], c_recv.at[level, part]).wait_recv()

    def ready(level, part):
        def tap(t, _):
            for half in range(2):
                for o in range(0, 32, 2):
                    pair = [
                        w_all[half, level, (o + k) % 4, (o + k) // 4, t].astype(F32) for k in range(2)
                    ]
                    w_tap[t, o * 8 : o * 8 + 16, half * HALF : (half + 1) * HALF] = jnp.concatenate(
                        pair, axis=0
                    ).astype(BF16)
            return 0

        lax.fori_loop(4 * part, 9 if part else 4, tap, 0)

    def products(pick, part, start):
        total = start
        for t in range(9)[SPLIT if part else DIRECT]:
            term = lax.dot_general(
                pick(t // 3, t % 3), w_tap[t], (((1,), (1,)), ((), ())), preferred_element_type=F32
            )
            total = term if total is None else total + term
        return total

    def conv3(part):
        def step(image, _):
            total = products(
                lambda kh, kw: x3[kw, image, kh : kh + 4].reshape(4 * 128, C),
                part,
                f3[image].reshape(4 * 128, C) if part else None,
            )
            f3[image] = total.reshape(4, 128, C)
            if part:
                sums[0, pl.ds(image, 1)] = jnp.sum(total, axis=0, keepdims=True)
                sums[1, pl.ds(image, 1)] = jnp.sum(total * total, axis=0, keepdims=True)
            return 0

        return step

    def conv_small(level, part, source, target):
        rows, width = LEVELS[level]
        ready(level, part)
        total = products(
            lambda kh, kw: source[kw, :, kh : kh + rows].reshape(B * rows * width, C),
            part,
            target[...].reshape(B * rows * width, C) if part else None,
        )
        target[...] = total.reshape(B, rows, width, C)
        for image in range(B if part else 0):
            one = total[image * rows * width : (image + 1) * rows * width]
            sums[2 * level, image : image + 1] = jnp.sum(one, axis=0, keepdims=True)
            sums[2 * level + 1, image : image + 1] = jnp.sum(one * one, axis=0, keepdims=True)

    after_z(0, 1)
    with jax.named_scope("s7_halo"):
        for level, held in ((2, h5), (1, h4), (0, h3)):
            all_of(held, halo_send.at[level], halo_recv.at[level]).wait_recv()
    lax.fori_loop(0, 1, outer, 0)
    after_z(0, 0)
    lax.fori_loop(1, 2, outer, 0)
    after_z(1, 1)
    lax.fori_loop(2, B, outer, 0)
    after_x(0, 1)
    after_z(1, 0)
    after_x(0, 0)
    after_z(2, 1)
    after_x(1, 1)
    after_z(2, 0)
    receive_partner(0, 0)
    with jax.named_scope("conv3Aa"):
        ready(0, 0)
        lax.fori_loop(0, 2, conv3(0), 0)
    after_x(1, 0)
    with jax.named_scope("conv3Ab"):
        lax.fori_loop(2, B, conv3(0), 0)
    after_y(0)
    after_x(2, 1)
    receive_partner(0, 1)
    with jax.named_scope("conv3Ca"):
        ready(0, 1)
        lax.fori_loop(0, 2, conv3(1), 0)
    after_x(2, 0)
    after_y(1)
    with jax.named_scope("conv3Cb"):
        lax.fori_loop(2, B, conv3(1), 0)
    receive_partner(1, 0)
    with jax.named_scope("conv4A"):
        conv_small(1, 0, x4, f4)
    after_y(2)
    receive_partner(1, 1)
    with jax.named_scope("conv4C"):
        conv_small(1, 1, x4, f4)
    receive_partner(2, 0)
    receive_partner(2, 1)
    with jax.named_scope("conv5"):
        conv_small(2, 0, x5, f5)
        conv_small(2, 1, x5, f5)

    channel = lax.broadcasted_iota(jnp.int32, (C, 128), 0)
    lane = lax.broadcasted_iota(jnp.int32, (C, 128), 1)
    member = lax.shift_right_logical(channel, 3)

    def selector(image):
        return (lane == member + 32 * image).astype(F32)

    packed = jnp.zeros((8, 128), F32)
    for image in range(B):
        packed += lax.dot_general(
            sums[:, image], selector(image), (((1,), (0,)), ((), ())),
            precision=lax.Precision.HIGHEST, preferred_element_type=F32,
        )
    stat_a[slot] = packed
    for who in ring_ids:
        remote(stat_a.at[slot], stat_a.at[slot], stat_send.at[0], stat_recv.at[0], who)
    with jax.named_scope("u1_stat"):
        all_of(stat_a.at[0:7], stat_send.at[0], stat_recv.at[0]).wait_recv()
    stat_b[x] = jnp.sum(stat_a[...], axis=0)
    for who in x_ids:
        remote(stat_b.at[x], stat_b.at[x], stat_send.at[1], stat_recv.at[1], who)
    with jax.named_scope("u2_stat"):
        all_of(stat_b.at[0:3], stat_send.at[1], stat_recv.at[1]).wait_recv()
    whole = jnp.sum(stat_b[...], axis=0)

    with jax.named_scope("v1_table"):
        pltpu.make_async_copy(params, params, local_sem.at[4]).wait()
        spreads = []
        for level, (rows, width) in enumerate(LEVELS):
            volume = float(rows * STRIPS * width * (C // G))
            mean = whole[2 * level : 2 * level + 1] / volume
            square = whole[2 * level + 1 : 2 * level + 2] / volume
            spread = jnp.maximum(square - mean * mean, 0.0)
            spreads += [mean, lax.rsqrt(spread + epsilon)]
        spreads += [jnp.zeros((2, 128), F32)]
        table = jnp.concatenate(spreads, axis=0)
        for image in range(B):
            spread_out = lax.dot_general(
                table, selector(image), (((1,), (1,)), ((), ())),
                precision=lax.Precision.HIGHEST, preferred_element_type=F32,
            )
            for level in range(3):
                table_ref[level, 0, image : image + 1] = spread_out[2 * level : 2 * level + 1]
                table_ref[level, 1, image : image + 1] = (
                    spread_out[2 * level + 1 : 2 * level + 2] * params[2 * level]
                )
                table_ref[level, 2, image : image + 1] = params[2 * level + 1]

    with jax.named_scope("v2_sends"):
        all_of(raw.at[0:7], raw_send.at[0], raw_recv.at[0]).wait_send()
        for level, held in ((2, h5), (1, h4), (0, h3)):
            all_of(held, halo_send.at[level], halo_recv.at[level]).wait_send()
        all_of(w_all.at[c, :, 0, 0:7], z_send.at[0], z_recv.at[0, 0]).wait_send()
        all_of(w_all.at[c, :, 0:3, :, DIRECT], x_send.at[0], x_recv.at[0, 0]).wait_send()
        all_of(w_all.at[c, :, 0:3, 0:2, SPLIT], x_send.at[1], x_recv.at[0, 1]).wait_send()
        all_of(w_all.at[c, :, 0:3, 0:6, SPLIT], y_send.at[0], y_recv.at[0]).wait_send()
        all_of(w_all.at[c], c_send.at[0], c_recv.at[0, 0]).wait_send()
        all_of(stat_a.at[0:7], stat_send.at[0], stat_recv.at[0]).wait_send()
        all_of(stat_b.at[0:3], stat_send.at[1], stat_recv.at[1]).wait_send()


def finish(f3, f4, f5, table, o3, o4, o5, s3, s4, s5, sem):
    copies = []
    for level, (source, held, target) in enumerate(((f3, s3, o3), (f4, s4, o4), (f5, s5, o5))):
        for image in range(B):
            center = table[level, 0, image : image + 1][None]
            scale = table[level, 1, image : image + 1][None]
            shift = table[level, 2, image : image + 1][None]
            held[image] = (source[image] - center) * scale + shift
            copy = pltpu.make_async_copy(held.at[image], target.at[image], sem.at[level, image])
            copy.start()
            copies.append(copy)
    for copy in copies:
        copy.wait()


def local(
    lateral3, lateral4, lateral5, conv_weight3, conv_weight4, conv_weight5,
    norm_gain3, norm_shift3, norm_gain4, norm_shift4, norm_gain5, norm_shift5,
):
    dma = pltpu.SemaphoreType.DMA
    vmem = pl.BlockSpec(memory_space=pltpu.VMEM)
    hbm = pl.BlockSpec(memory_space=pltpu.HBM)
    shapes = [jax.ShapeDtypeStruct((B, r, w, C), F32) for r, w in LEVELS]
    operands = [lateral3, lateral4, lateral5]
    operands += [w.reshape(3, 3, C) for w in (conv_weight3, conv_weight4, conv_weight5)]
    operands += [
        v.reshape(1, C)
        for v in (norm_gain3, norm_shift3, norm_gain4, norm_shift4, norm_gain5, norm_shift5)
    ]
    filtered = pl.pallas_call(
        kernel,
        out_shape=shapes + [jax.ShapeDtypeStruct((3, 3, B, C), F32)],
        in_specs=[hbm] * 12,
        out_specs=[vmem] * 4,
        scratch_shapes=[
            pltpu.VMEM((2, 3, NX, NZ, 9, 8, HALF), BF16),
            pltpu.VMEM((9, C, C), BF16),
            pltpu.VMEM((8, 3, 3, 3, HALF), BF16),
            pltpu.VMEM((B, 4, 128, C), BF16),
            pltpu.VMEM((B, 2, 64, C), BF16),
            pltpu.VMEM((B, 1, 32, C), BF16),
            pltpu.VMEM((2, B, 128, C), BF16),
            pltpu.VMEM((2, B, 64, C), BF16),
            pltpu.VMEM((2, B, 32, C), BF16),
            pltpu.VMEM((3, B, 6, 128, C), BF16),
            pltpu.VMEM((3, B, 4, 64, C), BF16),
            pltpu.VMEM((3, B, 3, 32, C), BF16),
            pltpu.VMEM((8, B, C), F32),
            pltpu.VMEM((8, 8, 128), F32),
            pltpu.VMEM((NX, 8, 128), F32),
            pltpu.VMEM((6, 1, C), F32),
            dma((5,)),
            dma((1,)), dma((3,)),
            dma((1,)), dma((3, 2)),
            dma((2,)), dma((3, 2)),
            dma((1,)), dma((3,)),
            dma((1,)), dma((3, 2)),
            dma((3,)), dma((3,)),
            dma((2,)), dma((2,)),
        ],
        compiler_params=pltpu.CompilerParams(
            collective_id=0, has_side_effects=True, vmem_limit_bytes=40 * 2**20
        ),
        name="neck",
    )(*(pltpu.with_memory_space_constraint(a, pltpu.HBM) for a in operands))

    return tuple(
        pl.pallas_call(
            finish,
            out_shape=shapes,
            in_specs=[vmem] * 4,
            out_specs=[hbm] * 3,
            scratch_shapes=[pltpu.VMEM(s.shape, F32) for s in shapes] + [dma((3, B))],
            compiler_params=pltpu.CompilerParams(vmem_limit_bytes=16 * 2**20),
            name="finish",
        )(*filtered)
    )


def solution(mesh):
    torus = Mesh(mesh.devices.reshape(NZ, NX, NY, NC), AXES)
    strips = P("z", SPACE, None, None)
    kernels = P(None, None, None, AXES)
    return jax.shard_map(
        local,
        mesh=torus,
        in_specs=(strips,) * 3 + (kernels,) * 3 + (P(),) * 6,
        out_specs=(strips,) * 3,
        check_vma=False,
    )
```

```python
import jax
import jax.numpy as jnp
from jax import lax
from jax.experimental import pallas as pl
from jax.experimental.pallas import tpu as pltpu
from jax.sharding import Mesh
from jax.sharding import PartitionSpec as P

SPACE = ("x", "y", "c")
AXES = ("z", "x", "y", "c")
MESH = pl.DeviceIdType.MESH
NZ, NX, NY, NC = 8, 4, 4, 2
STRIPS = NX * NY * NC
C, G, B = 256, 32, 4
HALF = 128
LEVELS = ((4, 128), (2, 64), (1, 32))
epsilon = 1e-05
F32, BF16 = jnp.float32, jnp.bfloat16


def wrap(value, size):
    return lax.rem(value + 2 * size, size)


def put(ref, image, row, value):
    n = value.shape[0]
    rounded = value.astype(BF16)
    wide = rounded.astype(F32)
    place = lax.broadcasted_iota(jnp.int32, wide.shape, 0)
    ref[1, image, row] = rounded
    ref[0, image, row] = jnp.where(place == 0, 0.0, pltpu.roll(wide, 1, 0)).astype(BF16)
    ref[2, image, row] = jnp.where(place == n - 1, 0.0, pltpu.roll(wide, n - 1, 0)).astype(BF16)


def repeat_matrix(n):
    rows = lax.broadcasted_iota(jnp.int32, (2 * n, n), 0)
    columns = lax.broadcasted_iota(jnp.int32, (2 * n, n), 1)
    return (lax.shift_right_logical(rows, 1) == columns).astype(F32).astype(BF16)


def kernel(
    lat3, lat4, lat5, w3, w4, w5, g3, b3, g4, b4, g5, b5,
    f3, f4, f5, table_ref,
    w_all, w_tap, raw, l3, l4, l5, h3, h4, h5, x3, x4, x5, sums, stat_a, stat_b, params,
    local_sem, raw_send, raw_recv, z_send, z_recv, x_send, x_recv, y_send, y_recv, c_send, c_recv,
    halo_send, halo_recv, stat_send, stat_recv,
):
    z, x, y, c = (lax.axis_index(a) for a in AXES)
    slot = y * 2 + c
    other = 1 - c
    strip = (x * NY + y) * 2 + c
    nxt, prv = wrap(strip + 1, STRIPS), wrap(strip - 1, STRIPS)
    next_id = (z, nxt // 8, lax.rem(nxt // 2, 4), lax.rem(nxt, 2))
    prev_id = (z, prv // 8, lax.rem(prv // 2, 4), lax.rem(prv, 2))
    partner = (z, x, y, other)

    ring_ids = [(z, x, wrap(y + dy, NY), k) for dy in (1, 2, 3) for k in range(2)] + [partner]
    y_ids = [(z, x, wrap(y + d, NY), c) for d in (1, 2, 3)]
    x_ids = [(z, wrap(x + d, NX), y, c) for d in (1, 2, 3)]
    z_ids = [(wrap(z + d, NZ), x, y, c) for d in range(1, NZ)]

    barrier = pltpu.get_barrier_semaphore()
    greeted = z_ids + x_ids + ring_ids + [next_id, prev_id]
    for who in greeted:
        pl.semaphore_signal(barrier, 1, device_id=who, device_id_type=MESH)

    loads = [
        pltpu.make_async_copy(lat5, l5, local_sem.at[0]),
        pltpu.make_async_copy(lat4, l4, local_sem.at[1]),
        pltpu.make_async_copy(lat3, l3, local_sem.at[2]),
    ]
    for copy in loads:
        copy.start()
    weights = (w3, w4, w5)
    mine = pl.ds(pl.multiple_of(c * HALF, HALF), HALF)
    theirs = pl.ds(pl.multiple_of(other * HALF, HALF), HALF)
    for level in range(3):
        pltpu.make_async_copy(
            weights[level].at[:, :, mine], raw.at[slot, level], local_sem.at[3]
        ).start()
    for i, source in enumerate((g3, b3, g4, b4, g5, b5)):
        pltpu.make_async_copy(source, params.at[i], local_sem.at[4]).start()

    def remote(source, target, sends, recvs, who):
        pltpu.make_async_remote_copy(
            source, target, sends, recvs, device_id=who, device_id_type=MESH
        ).start()

    def all_of(total, sends, recvs):
        return pltpu.make_async_remote_copy(
            total, total, sends, recvs, device_id=partner, device_id_type=MESH
        )

    with jax.named_scope("s3_barrier"):
        pl.semaphore_wait(barrier, len(greeted))

    for level in range(3):
        for dy in (2, 1, 3):
            for k in range(2):
                remote(
                    weights[level].at[:, :, k * HALF : (k + 1) * HALF], raw.at[slot, level],
                    raw_send.at[0], raw_recv.at[level], (z, x, wrap(y + dy, NY), k),
                )
        remote(
            weights[level].at[:, :, theirs], raw.at[slot, level],
            raw_send.at[0], raw_recv.at[level], partner,
        )

    for level, lateral, held, lowest in ((2, lat5, h5, 0), (1, lat4, h4, 1), (0, lat3, h3, 3)):
        remote(lateral.at[:, lowest], held.at[0], halo_send.at[level], halo_recv.at[level], next_id)
        remote(lateral.at[:, 0], held.at[1], halo_send.at[level], halo_recv.at[level], prev_id)

    first = strip == 0
    last = strip == STRIPS - 1
    up5, up4 = repeat_matrix(32), repeat_matrix(64)

    def rows5(image, row, source, hidden=None):
        value = source.astype(F32)
        if hidden is not None:
            value = jnp.where(hidden, 0.0, value)
        put(x5, image, row, value)

    def rows4(image, row, source, coarse, hidden=None):
        value = source.astype(F32) + jnp.dot(up5, coarse, preferred_element_type=F32)
        if hidden is not None:
            value = jnp.where(hidden, 0.0, value)
        put(x4, image, row, value)

    def rows3(image, row, source, hidden=None):
        middle = x4[1, image, (row + 1) // 2]
        value = source.astype(F32) + jnp.dot(up4, middle, preferred_element_type=F32)
        if hidden is not None:
            value = jnp.where(hidden, 0.0, value)
        put(x3, image, row, value)

    for copy in loads:
        copy.wait()

    def own(image, _):
        rows5(image, 1, l5[image, 0])
        for q in (1, 2):
            rows4(image, q, l4[image, q - 1], l5[image, 0])
        for r in (1, 2, 3, 4):
            rows3(image, r, l3[image, r - 1])
        return 0

    with jax.named_scope("s5_own"):
        lax.fori_loop(0, B, own, 0)

    DIRECT, SPLIT = slice(0, 4), slice(4, 9)
    quarter = pl.ds(2 * y, 2)
    pltpu.make_async_copy(raw.at[0], raw.at[0], local_sem.at[3]).wait()

    for level in range(3):
        with jax.named_scope(f"s6_raw{level}"):
            all_of(raw.at[0:7, level], raw_send.at[0], raw_recv.at[level]).wait_recv()
        for kh in range(3):
            rows = [raw[s, level, kh].astype(F32) for s in range(8)]
            for kw in range(3):
                tile = jnp.concatenate([r[kw : kw + 1] for r in rows], axis=0)
                w_all[c, level, x, z, kh * 3 + kw] = tile.astype(BF16)
        for block, part in (((0, 1),), ((1, 1), (0, 0)), ((2, 1), (1, 0), (2, 0)))[level]:
            for d in (4, 3, 5, 2, 6, 1, 7):
                ref = w_all.at[c, block, x, z, SPLIT if part else DIRECT]
                remote(ref, ref, z_send.at[0], z_recv.at[block, part], z_ids[d - 1])

    def outer(image, _):
        rows5(image, 0, h5[0, image], first)
        rows5(image, 2, h5[1, image], last)
        rows4(image, 0, h4[0, image], h5[0, image], first)
        rows4(image, 3, h4[1, image], h5[1, image], last)
        rows3(image, 0, h3[0, image], first)
        rows3(image, 5, h3[1, image], last)
        return 0

    def to_partner(level, part, ref):
        remote(ref, ref, c_send.at[0], c_recv.at[level, part], partner)

    def after_z(level, part):
        taps = SPLIT if part else DIRECT
        with jax.named_scope(f"z{level}{part}"):
            all_of(w_all.at[c, level, x, 0:7, taps], z_send.at[0], z_recv.at[level, part]).wait_recv()
        ref = w_all.at[c, level, x, quarter, taps] if part else w_all.at[c, level, x, :, taps]
        for d in (2, 1, 3):
            remote(ref, ref, x_send.at[part], x_recv.at[level, part], x_ids[d - 1])
        to_partner(level, part, w_all.at[c, level, x, :, taps])

    def after_x(level, part):
        with jax.named_scope(f"x{level}{part}"):
            if part:
                total = w_all.at[c, level, 0:3, 0:2, SPLIT]
            else:
                total = w_all.at[c, level, 0:3, :, DIRECT]
            all_of(total, x_send.at[part], x_recv.at[level, part]).wait_recv()
        for d in (1, 3, 2):
            where = wrap(x - d, NX)
            if part:
                ref = w_all.at[c, level, where, quarter, SPLIT]
                for e in (2, 1, 3):
                    remote(ref, ref, y_send.at[0], y_recv.at[level], y_ids[e - 1])
            else:
                to_partner(level, part, w_all.at[c, level, where, :, DIRECT])

    def after_y(level):
        with jax.named_scope(f"y{level}"):
            all_of(w_all.at[c, level, 0:3, 0:6, SPLIT], y_send.at[0], y_recv.at[level]).wait_recv()
        for d in (1, 2, 3):
            to_partner(level, 1, w_all.at[c, level, wrap(x - d, NX), :, SPLIT])

    def receive_partner(level, part):
        taps = SPLIT if part else DIRECT
        with jax.named_scope(f"c{level}{part}"):
            all_of(w_all.at[other, level, :, :, taps], c_send.at[0], c_recv.at[level, part]).wait_recv()

    def ready(level, part):
        def tap(t, _):
            for half in range(2):
                for o in range(0, 32, 2):
                    pair = [
                        w_all[half, level, (o + k) % 4, (o + k) // 4, t].astype(F32) for k in range(2)
                    ]
                    w_tap[t, o * 8 : o * 8 + 16, half * HALF : (half + 1) * HALF] = jnp.concatenate(
                        pair, axis=0
                    ).astype(BF16)
            return 0

        lax.fori_loop(4 * part, 9 if part else 4, tap, 0)

    def products(pick, part, start):
        total = start
        for t in range(9)[SPLIT if part else DIRECT]:
            term = lax.dot_general(
                pick(t // 3, t % 3), w_tap[t], (((1,), (1,)), ((), ())), preferred_element_type=F32
            )
            total = term if total is None else total + term
        return total

    def conv3(part):
        def step(image, _):
            total = products(
                lambda kh, kw: x3[kw, image, kh : kh + 4].reshape(4 * 128, C),
                part,
                f3[image].reshape(4 * 128, C) if part else None,
            )
            f3[image] = total.reshape(4, 128, C)
            if part:
                sums[0, pl.ds(image, 1)] = jnp.sum(total, axis=0, keepdims=True)
                sums[1, pl.ds(image, 1)] = jnp.sum(total * total, axis=0, keepdims=True)
            return 0

        return step

    def conv_small(level, part, source, target):
        rows, width = LEVELS[level]
        ready(level, part)
        total = products(
            lambda kh, kw: source[kw, :, kh : kh + rows].reshape(B * rows * width, C),
            part,
            target[...].reshape(B * rows * width, C) if part else None,
        )
        target[...] = total.reshape(B, rows, width, C)
        for image in range(B if part else 0):
            one = total[image * rows * width : (image + 1) * rows * width]
            sums[2 * level, image : image + 1] = jnp.sum(one, axis=0, keepdims=True)
            sums[2 * level + 1, image : image + 1] = jnp.sum(one * one, axis=0, keepdims=True)

    with jax.named_scope("s7_halo"):
        for level, held in ((2, h5), (1, h4), (0, h3)):
            all_of(held, halo_send.at[level], halo_recv.at[level]).wait_recv()
    lax.fori_loop(0, 2, outer, 0)
    after_z(0, 1)
    after_z(1, 1)
    after_z(0, 0)
    after_x(0, 1)
    after_z(2, 1)
    after_x(1, 1)
    lax.fori_loop(2, B, outer, 0)
    after_z(1, 0)
    after_z(2, 0)
    after_x(0, 0)
    after_x(2, 1)
    receive_partner(0, 0)
    with jax.named_scope("conv3Aa"):
        ready(0, 0)
        lax.fori_loop(0, 2, conv3(0), 0)
    after_y(0)
    with jax.named_scope("conv3Ab"):
        lax.fori_loop(2, B, conv3(0), 0)
    after_x(1, 0)
    receive_partner(0, 1)
    with jax.named_scope("conv3Ca"):
        ready(0, 1)
        lax.fori_loop(0, 2, conv3(1), 0)
    after_y(1)
    with jax.named_scope("conv3Cb"):
        lax.fori_loop(2, B, conv3(1), 0)
    after_x(2, 0)
    receive_partner(1, 0)
    with jax.named_scope("conv4A"):
        conv_small(1, 0, x4, f4)
    after_y(2)
    receive_partner(1, 1)
    with jax.named_scope("conv4C"):
        conv_small(1, 1, x4, f4)
    for part in (0, 1):
        receive_partner(2, part)
        with jax.named_scope(f"conv5{part}"):
            conv_small(2, part, x5, f5)

    def terms(value):
        high = value.astype(BF16)
        rest = value - high.astype(F32)
        middle = rest.astype(BF16)
        low = (rest - middle.astype(F32)).astype(BF16)
        return jnp.concatenate([high.astype(F32), middle.astype(F32), low.astype(F32)], axis=0).astype(BF16)

    channel = lax.broadcasted_iota(jnp.int32, (C, 128), 0)
    lane = lax.broadcasted_iota(jnp.int32, (C, 128), 1)
    member = (jnp.bitwise_and(lane, 31) == lax.shift_right_logical(channel, 3)).astype(F32).astype(BF16)
    owner = lax.shift_right_logical(lax.broadcasted_iota(jnp.int32, (8, 128), 1), 5)

    flat = jnp.concatenate([sums[:, image] for image in range(B)], axis=0)
    grouped = jnp.dot(terms(flat), member, preferred_element_type=F32)
    grouped = grouped[0:32] + grouped[32:64] + grouped[64:96]
    packed = jnp.zeros((8, 128), F32)
    for image in range(B):
        packed = jnp.where(owner == image, grouped[8 * image : 8 * image + 8], packed)
    stat_a[slot] = packed
    for who in ring_ids:
        remote(stat_a.at[slot], stat_a.at[slot], stat_send.at[0], stat_recv.at[0], who)
    with jax.named_scope("u1_stat"):
        all_of(stat_a.at[0:7], stat_send.at[0], stat_recv.at[0]).wait_recv()
    stat_b[x] = jnp.sum(stat_a[...], axis=0)
    for who in x_ids:
        remote(stat_b.at[x], stat_b.at[x], stat_send.at[1], stat_recv.at[1], who)
    with jax.named_scope("u2_stat"):
        all_of(stat_b.at[0:3], stat_send.at[1], stat_recv.at[1]).wait_recv()
    whole = jnp.sum(stat_b[...], axis=0)

    with jax.named_scope("v1_table"):
        pltpu.make_async_copy(params, params, local_sem.at[4]).wait()
        spreads = []
        for level, (rows, width) in enumerate(LEVELS):
            volume = float(rows * STRIPS * width * (C // G))
            mean = whole[2 * level : 2 * level + 1] / volume
            square = whole[2 * level + 1 : 2 * level + 2] / volume
            spread = jnp.maximum(square - mean * mean, 0.0)
            spreads += [mean, lax.rsqrt(spread + epsilon)]
        spreads += [jnp.zeros((2, 128), F32)]
        table = jnp.concatenate(spreads, axis=0)
        chosen = jnp.concatenate(
            [jnp.where(owner == image, table, 0.0) for image in range(B)], axis=0
        )
        wide = lax.dot_general(
            terms(chosen), member, (((1,), (1,)), ((), ())), preferred_element_type=F32
        )
        wide = wide[0:32] + wide[32:64] + wide[64:96]
        for image in range(B):
            spread_out = wide[8 * image : 8 * image + 8]
            for level in range(3):
                table_ref[level, 0, image : image + 1] = spread_out[2 * level : 2 * level + 1]
                table_ref[level, 1, image : image + 1] = (
                    spread_out[2 * level + 1 : 2 * level + 2] * params[2 * level]
                )
                table_ref[level, 2, image : image + 1] = params[2 * level + 1]

    with jax.named_scope("v2_sends"):
        all_of(raw.at[0:7], raw_send.at[0], raw_recv.at[0]).wait_send()
        for level, held in ((2, h5), (1, h4), (0, h3)):
            all_of(held, halo_send.at[level], halo_recv.at[level]).wait_send()
        all_of(w_all.at[c, :, 0, 0:7], z_send.at[0], z_recv.at[0, 0]).wait_send()
        all_of(w_all.at[c, :, 0:3, :, DIRECT], x_send.at[0], x_recv.at[0, 0]).wait_send()
        all_of(w_all.at[c, :, 0:3, 0:2, SPLIT], x_send.at[1], x_recv.at[0, 1]).wait_send()
        all_of(w_all.at[c, :, 0:3, 0:6, SPLIT], y_send.at[0], y_recv.at[0]).wait_send()
        all_of(w_all.at[c], c_send.at[0], c_recv.at[0, 0]).wait_send()
        all_of(stat_a.at[0:7], stat_send.at[0], stat_recv.at[0]).wait_send()
        all_of(stat_b.at[0:3], stat_send.at[1], stat_recv.at[1]).wait_send()


def finish(f3, f4, f5, table, o3, o4, o5, s3, s4, s5, sem):
    copies = []
    for level, (source, held, target) in enumerate(((f3, s3, o3), (f4, s4, o4), (f5, s5, o5))):
        for image in range(B):
            center = table[level, 0, image : image + 1][None]
            scale = table[level, 1, image : image + 1][None]
            shift = table[level, 2, image : image + 1][None]
            held[image] = (source[image] - center) * scale + shift
            copy = pltpu.make_async_copy(held.at[image], target.at[image], sem.at[level, image])
            copy.start()
            copies.append(copy)
    for copy in copies:
        copy.wait()


def local(
    lateral3, lateral4, lateral5, conv_weight3, conv_weight4, conv_weight5,
    norm_gain3, norm_shift3, norm_gain4, norm_shift4, norm_gain5, norm_shift5,
):
    dma = pltpu.SemaphoreType.DMA
    vmem = pl.BlockSpec(memory_space=pltpu.VMEM)
    hbm = pl.BlockSpec(memory_space=pltpu.HBM)
    shapes = [jax.ShapeDtypeStruct((B, r, w, C), F32) for r, w in LEVELS]
    operands = [lateral3, lateral4, lateral5]
    operands += [w.reshape(3, 3, C) for w in (conv_weight3, conv_weight4, conv_weight5)]
    operands += [
        v.reshape(1, C)
        for v in (norm_gain3, norm_shift3, norm_gain4, norm_shift4, norm_gain5, norm_shift5)
    ]
    filtered = pl.pallas_call(
        kernel,
        out_shape=shapes + [jax.ShapeDtypeStruct((3, 3, B, C), F32)],
        in_specs=[hbm] * 12,
        out_specs=[vmem] * 4,
        scratch_shapes=[
            pltpu.VMEM((2, 3, NX, NZ, 9, 8, HALF), BF16),
            pltpu.VMEM((9, C, C), BF16),
            pltpu.VMEM((8, 3, 3, 3, HALF), BF16),
            pltpu.VMEM((B, 4, 128, C), BF16),
            pltpu.VMEM((B, 2, 64, C), BF16),
            pltpu.VMEM((B, 1, 32, C), BF16),
            pltpu.VMEM((2, B, 128, C), BF16),
            pltpu.VMEM((2, B, 64, C), BF16),
            pltpu.VMEM((2, B, 32, C), BF16),
            pltpu.VMEM((3, B, 6, 128, C), BF16),
            pltpu.VMEM((3, B, 4, 64, C), BF16),
            pltpu.VMEM((3, B, 3, 32, C), BF16),
            pltpu.VMEM((8, B, C), F32),
            pltpu.VMEM((8, 8, 128), F32),
            pltpu.VMEM((NX, 8, 128), F32),
            pltpu.VMEM((6, 1, C), F32),
            dma((5,)),
            dma((1,)), dma((3,)),
            dma((1,)), dma((3, 2)),
            dma((2,)), dma((3, 2)),
            dma((1,)), dma((3,)),
            dma((1,)), dma((3, 2)),
            dma((3,)), dma((3,)),
            dma((2,)), dma((2,)),
        ],
        compiler_params=pltpu.CompilerParams(
            collective_id=0, has_side_effects=True, vmem_limit_bytes=40 * 2**20
        ),
        name="neck",
    )(*(pltpu.with_memory_space_constraint(a, pltpu.HBM) for a in operands))

    return tuple(
        pl.pallas_call(
            finish,
            out_shape=shapes,
            in_specs=[vmem] * 4,
            out_specs=[hbm] * 3,
            scratch_shapes=[pltpu.VMEM(s.shape, F32) for s in shapes] + [dma((3, B))],
            compiler_params=pltpu.CompilerParams(vmem_limit_bytes=16 * 2**20),
            name="finish",
        )(*filtered)
    )


def solution(mesh):
    torus = Mesh(mesh.devices.reshape(NZ, NX, NY, NC), AXES)
    strips = P("z", SPACE, None, None)
    kernels = P(None, None, None, AXES)
    return jax.shard_map(
        local,
        mesh=torus,
        in_specs=(strips,) * 3 + (kernels,) * 3 + (P(),) * 6,
        out_specs=(strips,) * 3,
        check_vma=False,
    )
```

```python
import jax
import jax.numpy as jnp
from jax import lax
from jax.experimental import pallas as pl
from jax.experimental.pallas import tpu as pltpu
from jax.sharding import Mesh
from jax.sharding import PartitionSpec as P

SPACE = ("x", "y", "c")
AXES = ("z", "x", "y", "c")
MESH = pl.DeviceIdType.MESH
NZ, NX, NY, NC = 8, 4, 4, 2
STRIPS = NX * NY * NC
C, G, B = 256, 32, 4
HALF = 128
LEVELS = ((4, 128), (2, 64), (1, 32))
epsilon = 1e-05
F32, BF16 = jnp.float32, jnp.bfloat16


def wrap(value, size):
    return lax.rem(value + 2 * size, size)


def put(ref, image, row, value):
    n = value.shape[0]
    rounded = value.astype(BF16)
    wide = rounded.astype(F32)
    place = lax.broadcasted_iota(jnp.int32, wide.shape, 0)
    ref[1, image, row] = rounded
    ref[0, image, row] = jnp.where(place == 0, 0.0, pltpu.roll(wide, 1, 0)).astype(BF16)
    ref[2, image, row] = jnp.where(place == n - 1, 0.0, pltpu.roll(wide, n - 1, 0)).astype(BF16)


def repeat_matrix(n):
    rows = lax.broadcasted_iota(jnp.int32, (2 * n, n), 0)
    columns = lax.broadcasted_iota(jnp.int32, (2 * n, n), 1)
    return (lax.shift_right_logical(rows, 1) == columns).astype(F32).astype(BF16)


def kernel(
    lat3, lat4, lat5, w3, w4, w5, g3, b3, g4, b4, g5, b5,
    f3, f4, f5, table_ref,
    w_all, w_tap, raw, l3, l4, l5, h3, h4, h5, x3, x4, x5, sums, stat_a, stat_b, params,
    local_sem, raw_send, raw_recv, z_send, z_recv, x_send, x_recv, y_send, y_recv, c_send, c_recv,
    halo_send, halo_recv, stat_send, stat_recv,
):
    z, x, y, c = (lax.axis_index(a) for a in AXES)
    slot = y * 2 + c
    other = 1 - c
    strip = (x * NY + y) * 2 + c
    nxt, prv = wrap(strip + 1, STRIPS), wrap(strip - 1, STRIPS)
    next_id = (z, nxt // 8, lax.rem(nxt // 2, 4), lax.rem(nxt, 2))
    prev_id = (z, prv // 8, lax.rem(prv // 2, 4), lax.rem(prv, 2))
    partner = (z, x, y, other)

    ring_ids = [(z, x, wrap(y + dy, NY), k) for dy in (1, 2, 3) for k in range(2)] + [partner]
    y_ids = [(z, x, wrap(y + d, NY), c) for d in (1, 2, 3)]
    x_ids = [(z, wrap(x + d, NX), y, c) for d in (1, 2, 3)]
    z_ids = [(wrap(z + d, NZ), x, y, c) for d in range(1, NZ)]

    barrier = pltpu.get_barrier_semaphore()
    greeted = z_ids + x_ids + ring_ids + [next_id, prev_id]
    for who in greeted:
        pl.semaphore_signal(barrier, 1, device_id=who, device_id_type=MESH)

    loads = [
        pltpu.make_async_copy(lat5, l5, local_sem.at[0]),
        pltpu.make_async_copy(lat4, l4, local_sem.at[1]),
        pltpu.make_async_copy(lat3, l3, local_sem.at[2]),
    ]
    for copy in loads:
        copy.start()
    weights = (w3, w4, w5)
    mine = pl.ds(pl.multiple_of(c * HALF, HALF), HALF)
    theirs = pl.ds(pl.multiple_of(other * HALF, HALF), HALF)
    for level in range(3):
        pltpu.make_async_copy(
            weights[level].at[:, :, mine], raw.at[slot, level], local_sem.at[3]
        ).start()
    for i, source in enumerate((g3, b3, g4, b4, g5, b5)):
        pltpu.make_async_copy(source, params.at[i], local_sem.at[4]).start()

    def remote(source, target, sends, recvs, who):
        pltpu.make_async_remote_copy(
            source, target, sends, recvs, device_id=who, device_id_type=MESH
        ).start()

    def all_of(total, sends, recvs):
        return pltpu.make_async_remote_copy(
            total, total, sends, recvs, device_id=partner, device_id_type=MESH
        )

    with jax.named_scope("s3_barrier"):
        pl.semaphore_wait(barrier, len(greeted))

    for level in range(3):
        for dy in (2, 1, 3):
            for k in range(2):
                remote(
                    weights[level].at[:, :, k * HALF : (k + 1) * HALF], raw.at[slot, level],
                    raw_send.at[0], raw_recv.at[level], (z, x, wrap(y + dy, NY), k),
                )
        remote(
            weights[level].at[:, :, theirs], raw.at[slot, level],
            raw_send.at[0], raw_recv.at[level], partner,
        )

    first = strip == 0
    last = strip == STRIPS - 1
    up5, up4 = repeat_matrix(32), repeat_matrix(64)

    def rows5(image, row, source, hidden=None):
        value = source.astype(F32)
        if hidden is not None:
            value = jnp.where(hidden, 0.0, value)
        put(x5, image, row, value)

    def rows4(image, row, source, coarse, hidden=None):
        value = source.astype(F32) + jnp.dot(up5, coarse, preferred_element_type=F32)
        if hidden is not None:
            value = jnp.where(hidden, 0.0, value)
        put(x4, image, row, value)

    def rows3(image, row, source, hidden=None):
        middle = x4[1, image, (row + 1) // 2]
        value = source.astype(F32) + jnp.dot(up4, middle, preferred_element_type=F32)
        if hidden is not None:
            value = jnp.where(hidden, 0.0, value)
        put(x3, image, row, value)

    for copy in loads:
        copy.wait()

    def own(image, _):
        rows5(image, 1, l5[image, 0])
        for q in (1, 2):
            rows4(image, q, l4[image, q - 1], l5[image, 0])
        for r in (1, 2, 3, 4):
            rows3(image, r, l3[image, r - 1])
        return 0

    with jax.named_scope("s5_own"):
        lax.fori_loop(0, B, own, 0)

    DIRECT, SPLIT = slice(0, 4), slice(4, 9)
    quarter = pl.ds(2 * y, 2)
    pltpu.make_async_copy(raw.at[0], raw.at[0], local_sem.at[3]).wait()

    for level in range(3):
        with jax.named_scope(f"s6_raw{level}"):
            all_of(raw.at[0:7, level], raw_send.at[0], raw_recv.at[level]).wait_recv()
        for kh in range(3):
            rows = [raw[s, level, kh].astype(F32) for s in range(8)]
            for kw in range(3):
                tile = jnp.concatenate([r[kw : kw + 1] for r in rows], axis=0)
                w_all[c, level, x, z, kh * 3 + kw] = tile.astype(BF16)
        for block, part in (((0, 1),), ((1, 1), (0, 0)), ((2, 1), (1, 0), (2, 0)))[level]:
            for d in (4, 3, 5, 2, 6, 1, 7):
                ref = w_all.at[c, block, x, z, SPLIT if part else DIRECT]
                remote(ref, ref, z_send.at[0], z_recv.at[block, part], z_ids[d - 1])

    for level, lateral, held, lowest in ((2, lat5, h5, 0), (1, lat4, h4, 1), (0, lat3, h3, 3)):
        remote(lateral.at[:, lowest], held.at[0], halo_send.at[level], halo_recv.at[level], next_id)
        remote(lateral.at[:, 0], held.at[1], halo_send.at[level], halo_recv.at[level], prev_id)

    def outer(image, _):
        rows5(image, 0, h5[0, image], first)
        rows5(image, 2, h5[1, image], last)
        rows4(image, 0, h4[0, image], h5[0, image], first)
        rows4(image, 3, h4[1, image], h5[1, image], last)
        rows3(image, 0, h3[0, image], first)
        rows3(image, 5, h3[1, image], last)
        return 0

    def to_partner(level, part, ref):
        remote(ref, ref, c_send.at[0], c_recv.at[level, part], partner)

    def after_z(level, part):
        taps = SPLIT if part else DIRECT
        with jax.named_scope(f"z{level}{part}"):
            all_of(w_all.at[c, level, x, 0:7, taps], z_send.at[0], z_recv.at[level, part]).wait_recv()
        ref = w_all.at[c, level, x, quarter, taps] if part else w_all.at[c, level, x, :, taps]
        for d in (2, 1, 3):
            remote(ref, ref, x_send.at[part], x_recv.at[level, part], x_ids[d - 1])
        to_partner(level, part, w_all.at[c, level, x, :, taps])

    def after_x(level, part):
        with jax.named_scope(f"x{level}{part}"):
            if part:
                total = w_all.at[c, level, 0:3, 0:2, SPLIT]
            else:
                total = w_all.at[c, level, 0:3, :, DIRECT]
            all_of(total, x_send.at[part], x_recv.at[level, part]).wait_recv()
        for d in (1, 3, 2):
            where = wrap(x - d, NX)
            if part:
                ref = w_all.at[c, level, where, quarter, SPLIT]
                for e in (2, 1, 3):
                    remote(ref, ref, y_send.at[0], y_recv.at[level], y_ids[e - 1])
            else:
                to_partner(level, part, w_all.at[c, level, where, :, DIRECT])

    def after_y(level):
        with jax.named_scope(f"y{level}"):
            all_of(w_all.at[c, level, 0:3, 0:6, SPLIT], y_send.at[0], y_recv.at[level]).wait_recv()
        for d in (1, 2, 3):
            to_partner(level, 1, w_all.at[c, level, wrap(x - d, NX), :, SPLIT])

    def receive_partner(level, part):
        taps = SPLIT if part else DIRECT
        with jax.named_scope(f"c{level}{part}"):
            all_of(w_all.at[other, level, :, :, taps], c_send.at[0], c_recv.at[level, part]).wait_recv()

    def ready(level, part):
        def tap(t, _):
            for half in range(2):
                for o in range(0, 32, 2):
                    pair = [
                        w_all[half, level, (o + k) % 4, (o + k) // 4, t].astype(F32) for k in range(2)
                    ]
                    w_tap[t, o * 8 : o * 8 + 16, half * HALF : (half + 1) * HALF] = jnp.concatenate(
                        pair, axis=0
                    ).astype(BF16)
            return 0

        lax.fori_loop(4 * part, 9 if part else 4, tap, 0)

    def products(pick, part, start):
        total = start
        for t in range(9)[SPLIT if part else DIRECT]:
            term = lax.dot_general(
                pick(t // 3, t % 3), w_tap[t], (((1,), (1,)), ((), ())), preferred_element_type=F32
            )
            total = term if total is None else total + term
        return total

    def conv3(part):
        def step(image, _):
            total = products(
                lambda kh, kw: x3[kw, image, kh : kh + 4].reshape(4 * 128, C),
                part,
                f3[image].reshape(4 * 128, C) if part else None,
            )
            f3[image] = total.reshape(4, 128, C)
            if part:
                sums[0, pl.ds(image, 1)] = jnp.sum(total, axis=0, keepdims=True)
                sums[1, pl.ds(image, 1)] = jnp.sum(total * total, axis=0, keepdims=True)
            return 0

        return step

    def conv_small(level, part, source, target):
        rows, width = LEVELS[level]
        ready(level, part)
        total = products(
            lambda kh, kw: source[kw, :, kh : kh + rows].reshape(B * rows * width, C),
            part,
            target[...].reshape(B * rows * width, C) if part else None,
        )
        target[...] = total.reshape(B, rows, width, C)
        for image in range(B if part else 0):
            one = total[image * rows * width : (image + 1) * rows * width]
            sums[2 * level, image : image + 1] = jnp.sum(one, axis=0, keepdims=True)
            sums[2 * level + 1, image : image + 1] = jnp.sum(one * one, axis=0, keepdims=True)

    after_z(0, 1)
    after_z(1, 1)
    after_z(0, 0)
    after_x(0, 1)
    with jax.named_scope("s7_halo"):
        for level, held in ((2, h5), (1, h4), (0, h3)):
            all_of(held, halo_send.at[level], halo_recv.at[level]).wait_recv()
    lax.fori_loop(0, 2, outer, 0)
    after_z(2, 1)
    after_x(1, 1)
    lax.fori_loop(2, B, outer, 0)
    after_z(1, 0)
    after_z(2, 0)
    after_x(0, 0)
    after_x(2, 1)
    receive_partner(0, 0)
    with jax.named_scope("conv3Aa"):
        ready(0, 0)
        lax.fori_loop(0, 2, conv3(0), 0)
    after_y(0)
    with jax.named_scope("conv3Ab"):
        lax.fori_loop(2, B, conv3(0), 0)
    after_x(1, 0)
    receive_partner(0, 1)
    with jax.named_scope("conv3Ca"):
        ready(0, 1)
        lax.fori_loop(0, 2, conv3(1), 0)
    after_y(1)
    with jax.named_scope("conv3Cb"):
        lax.fori_loop(2, B, conv3(1), 0)
    after_x(2, 0)
    receive_partner(1, 0)
    with jax.named_scope("conv4A"):
        conv_small(1, 0, x4, f4)
    after_y(2)
    receive_partner(1, 1)
    with jax.named_scope("conv4C"):
        conv_small(1, 1, x4, f4)
    for part in (0, 1):
        receive_partner(2, part)
        with jax.named_scope(f"conv5{part}"):
            conv_small(2, part, x5, f5)

    def terms(value):
        high = value.astype(BF16)
        rest = value - high.astype(F32)
        middle = rest.astype(BF16)
        low = (rest - middle.astype(F32)).astype(BF16)
        return jnp.concatenate([high.astype(F32), middle.astype(F32), low.astype(F32)], axis=0).astype(BF16)

    channel = lax.broadcasted_iota(jnp.int32, (C, 128), 0)
    lane = lax.broadcasted_iota(jnp.int32, (C, 128), 1)
    member = (jnp.bitwise_and(lane, 31) == lax.shift_right_logical(channel, 3)).astype(F32).astype(BF16)
    owner = lax.shift_right_logical(lax.broadcasted_iota(jnp.int32, (8, 128), 1), 5)

    flat = jnp.concatenate([sums[:, image] for image in range(B)], axis=0)
    grouped = jnp.dot(terms(flat), member, preferred_element_type=F32)
    grouped = grouped[0:32] + grouped[32:64] + grouped[64:96]
    packed = jnp.zeros((8, 128), F32)
    for image in range(B):
        packed = jnp.where(owner == image, grouped[8 * image : 8 * image + 8], packed)
    stat_a[slot] = packed
    for who in ring_ids:
        remote(stat_a.at[slot], stat_a.at[slot], stat_send.at[0], stat_recv.at[0], who)
    with jax.named_scope("u1_stat"):
        all_of(stat_a.at[0:7], stat_send.at[0], stat_recv.at[0]).wait_recv()
    stat_b[x] = jnp.sum(stat_a[...], axis=0)
    for who in x_ids:
        remote(stat_b.at[x], stat_b.at[x], stat_send.at[1], stat_recv.at[1], who)
    with jax.named_scope("u2_stat"):
        all_of(stat_b.at[0:3], stat_send.at[1], stat_recv.at[1]).wait_recv()
    whole = jnp.sum(stat_b[...], axis=0)

    with jax.named_scope("v1_table"):
        pltpu.make_async_copy(params, params, local_sem.at[4]).wait()
        spreads = []
        for level, (rows, width) in enumerate(LEVELS):
            volume = float(rows * STRIPS * width * (C // G))
            mean = whole[2 * level : 2 * level + 1] / volume
            square = whole[2 * level + 1 : 2 * level + 2] / volume
            spread = jnp.maximum(square - mean * mean, 0.0)
            spreads += [mean, lax.rsqrt(spread + epsilon)]
        spreads += [jnp.zeros((2, 128), F32)]
        table = jnp.concatenate(spreads, axis=0)
        chosen = jnp.concatenate(
            [jnp.where(owner == image, table, 0.0) for image in range(B)], axis=0
        )
        wide = lax.dot_general(
            terms(chosen), member, (((1,), (1,)), ((), ())), preferred_element_type=F32
        )
        wide = wide[0:32] + wide[32:64] + wide[64:96]
        for image in range(B):
            spread_out = wide[8 * image : 8 * image + 8]
            for level in range(3):
                table_ref[level, 0, image : image + 1] = spread_out[2 * level : 2 * level + 1]
                table_ref[level, 1, image : image + 1] = (
                    spread_out[2 * level + 1 : 2 * level + 2] * params[2 * level]
                )
                table_ref[level, 2, image : image + 1] = params[2 * level + 1]

    with jax.named_scope("v2_sends"):
        all_of(raw.at[0:7], raw_send.at[0], raw_recv.at[0]).wait_send()
        for level, held in ((2, h5), (1, h4), (0, h3)):
            all_of(held, halo_send.at[level], halo_recv.at[level]).wait_send()
        all_of(w_all.at[c, :, 0, 0:7], z_send.at[0], z_recv.at[0, 0]).wait_send()
        all_of(w_all.at[c, :, 0:3, :, DIRECT], x_send.at[0], x_recv.at[0, 0]).wait_send()
        all_of(w_all.at[c, :, 0:3, 0:2, SPLIT], x_send.at[1], x_recv.at[0, 1]).wait_send()
        all_of(w_all.at[c, :, 0:3, 0:6, SPLIT], y_send.at[0], y_recv.at[0]).wait_send()
        all_of(w_all.at[c], c_send.at[0], c_recv.at[0, 0]).wait_send()
        all_of(stat_a.at[0:7], stat_send.at[0], stat_recv.at[0]).wait_send()
        all_of(stat_b.at[0:3], stat_send.at[1], stat_recv.at[1]).wait_send()


def finish(f3, f4, f5, table, o3, o4, o5, s3, s4, s5, sem):
    copies = []
    for level, (source, held, target) in enumerate(((f3, s3, o3), (f4, s4, o4), (f5, s5, o5))):
        for image in range(B):
            center = table[level, 0, image : image + 1][None]
            scale = table[level, 1, image : image + 1][None]
            shift = table[level, 2, image : image + 1][None]
            held[image] = (source[image] - center) * scale + shift
            copy = pltpu.make_async_copy(held.at[image], target.at[image], sem.at[level, image])
            copy.start()
            copies.append(copy)
    for copy in copies:
        copy.wait()


def local(
    lateral3, lateral4, lateral5, conv_weight3, conv_weight4, conv_weight5,
    norm_gain3, norm_shift3, norm_gain4, norm_shift4, norm_gain5, norm_shift5,
):
    dma = pltpu.SemaphoreType.DMA
    vmem = pl.BlockSpec(memory_space=pltpu.VMEM)
    hbm = pl.BlockSpec(memory_space=pltpu.HBM)
    shapes = [jax.ShapeDtypeStruct((B, r, w, C), F32) for r, w in LEVELS]
    operands = [lateral3, lateral4, lateral5]
    operands += [w.reshape(3, 3, C) for w in (conv_weight3, conv_weight4, conv_weight5)]
    operands += [
        v.reshape(1, C)
        for v in (norm_gain3, norm_shift3, norm_gain4, norm_shift4, norm_gain5, norm_shift5)
    ]
    filtered = pl.pallas_call(
        kernel,
        out_shape=shapes + [jax.ShapeDtypeStruct((3, 3, B, C), F32)],
        in_specs=[hbm] * 12,
        out_specs=[vmem] * 4,
        scratch_shapes=[
            pltpu.VMEM((2, 3, NX, NZ, 9, 8, HALF), BF16),
            pltpu.VMEM((9, C, C), BF16),
            pltpu.VMEM((8, 3, 3, 3, HALF), BF16),
            pltpu.VMEM((B, 4, 128, C), BF16),
            pltpu.VMEM((B, 2, 64, C), BF16),
            pltpu.VMEM((B, 1, 32, C), BF16),
            pltpu.VMEM((2, B, 128, C), BF16),
            pltpu.VMEM((2, B, 64, C), BF16),
            pltpu.VMEM((2, B, 32, C), BF16),
            pltpu.VMEM((3, B, 6, 128, C), BF16),
            pltpu.VMEM((3, B, 4, 64, C), BF16),
            pltpu.VMEM((3, B, 3, 32, C), BF16),
            pltpu.VMEM((8, B, C), F32),
            pltpu.VMEM((8, 8, 128), F32),
            pltpu.VMEM((NX, 8, 128), F32),
            pltpu.VMEM((6, 1, C), F32),
            dma((5,)),
            dma((1,)), dma((3,)),
            dma((1,)), dma((3, 2)),
            dma((2,)), dma((3, 2)),
            dma((1,)), dma((3,)),
            dma((1,)), dma((3, 2)),
            dma((3,)), dma((3,)),
            dma((2,)), dma((2,)),
        ],
        compiler_params=pltpu.CompilerParams(
            collective_id=0, has_side_effects=True, vmem_limit_bytes=40 * 2**20
        ),
        name="neck",
    )(*(pltpu.with_memory_space_constraint(a, pltpu.HBM) for a in operands))

    return tuple(
        pl.pallas_call(
            finish,
            out_shape=shapes,
            in_specs=[vmem] * 4,
            out_specs=[hbm] * 3,
            scratch_shapes=[pltpu.VMEM(s.shape, F32) for s in shapes] + [dma((3, B))],
            compiler_params=pltpu.CompilerParams(vmem_limit_bytes=16 * 2**20),
            name="finish",
        )(*filtered)
    )


def solution(mesh):
    torus = Mesh(mesh.devices.reshape(NZ, NX, NY, NC), AXES)
    strips = P("z", SPACE, None, None)
    kernels = P(None, None, None, AXES)
    return jax.shard_map(
        local,
        mesh=torus,
        in_specs=(strips,) * 3 + (kernels,) * 3 + (P(),) * 6,
        out_specs=(strips,) * 3,
        check_vma=False,
    )
```

```python
import jax
import jax.numpy as jnp
from jax import lax
from jax.experimental import pallas as pl
from jax.experimental.pallas import tpu as pltpu
from jax.sharding import Mesh
from jax.sharding import PartitionSpec as P

SPACE = ("x", "y", "c")
AXES = ("z", "x", "y", "c")
MESH = pl.DeviceIdType.MESH
NZ, NX, NY, NC = 8, 4, 4, 2
STRIPS = NX * NY * NC
C, G, B = 256, 32, 4
HALF = 128
LEVELS = ((4, 128), (2, 64), (1, 32))
DIRECT_TAPS = (3, 3, 3)
epsilon = 1e-05
F32, BF16 = jnp.float32, jnp.bfloat16


def wrap(value, size):
    return lax.rem(value + 2 * size, size)


def put(ref, image, row, value):
    n = value.shape[0]
    rounded = value.astype(BF16)
    wide = rounded.astype(F32)
    place = lax.broadcasted_iota(jnp.int32, wide.shape, 0)
    ref[1, image, row] = rounded
    ref[0, image, row] = jnp.where(place == 0, 0.0, pltpu.roll(wide, 1, 0)).astype(BF16)
    ref[2, image, row] = jnp.where(place == n - 1, 0.0, pltpu.roll(wide, n - 1, 0)).astype(BF16)


def repeat_matrix(n):
    rows = lax.broadcasted_iota(jnp.int32, (2 * n, n), 0)
    columns = lax.broadcasted_iota(jnp.int32, (2 * n, n), 1)
    return (lax.shift_right_logical(rows, 1) == columns).astype(F32).astype(BF16)


def kernel(
    lat3, lat4, lat5, w3, w4, w5, g3, b3, g4, b4, g5, b5,
    f3, f4, f5, table_ref,
    w_all, w_tap, raw, l3, l4, l5, h3, h4, h5, x3, x4, x5, sums, stats, params,
    local_sem, raw_send, raw_recv, z_send, z_recv, x_send, x_recv, y_send, y_recv, c_send, c_recv,
    halo_send, halo_recv, stat_send, stat_recv,
):
    z, x, y, c = (lax.axis_index(a) for a in AXES)
    slot = y * 2 + c
    other = 1 - c
    strip = (x * NY + y) * 2 + c
    nxt, prv = wrap(strip + 1, STRIPS), wrap(strip - 1, STRIPS)
    next_id = (z, nxt // 8, lax.rem(nxt // 2, 4), lax.rem(nxt, 2))
    prev_id = (z, prv // 8, lax.rem(prv // 2, 4), lax.rem(prv, 2))
    partner = (z, x, y, other)

    ring_ids = [(z, x, wrap(y + dy, NY), k) for dy in (1, 2, 3) for k in range(2)] + [partner]
    y_ids = [(z, x, wrap(y + d, NY), c) for d in (1, 2, 3)]
    x_ids = [(z, wrap(x + d, NX), y, c) for d in (1, 2, 3)]
    z_ids = [(wrap(z + d, NZ), x, y, c) for d in range(1, NZ)]

    xs = [x] + [who[1] for who in x_ids]
    ys = [y] + [who[2] for who in y_ids]
    plane_ids = [
        (z, to_x, to_y, to_c)
        for i, to_x in enumerate(xs)
        for j, to_y in enumerate(ys)
        for k, to_c in enumerate((c, other))
        if i + j + k > 0
    ]

    barrier = pltpu.get_barrier_semaphore()
    greeted = z_ids + x_ids + ring_ids + [next_id, prev_id]
    for who in greeted:
        pl.semaphore_signal(barrier, 1, device_id=who, device_id_type=MESH)

    loads = [
        pltpu.make_async_copy(lat5, l5, local_sem.at[0]),
        pltpu.make_async_copy(lat4, l4, local_sem.at[1]),
        pltpu.make_async_copy(lat3, l3, local_sem.at[2]),
    ]
    for copy in loads:
        copy.start()
    weights = (w3, w4, w5)
    mine = pl.ds(pl.multiple_of(c * HALF, HALF), HALF)
    theirs = pl.ds(pl.multiple_of(other * HALF, HALF), HALF)
    for level in range(3):
        pltpu.make_async_copy(
            weights[level].at[:, :, mine], raw.at[slot, level], local_sem.at[3]
        ).start()
    for i, source in enumerate((g3, b3, g4, b4, g5, b5)):
        pltpu.make_async_copy(source, params.at[i], local_sem.at[4]).start()

    def remote(source, target, sends, recvs, who):
        pltpu.make_async_remote_copy(
            source, target, sends, recvs, device_id=who, device_id_type=MESH
        ).start()

    def all_of(total, sends, recvs):
        return pltpu.make_async_remote_copy(
            total, total, sends, recvs, device_id=partner, device_id_type=MESH
        )

    with jax.named_scope("s3_barrier"):
        pl.semaphore_wait(barrier, len(greeted))

    for level in range(3):
        for dy in (2, 1, 3):
            for k in range(2):
                remote(
                    weights[level].at[:, :, k * HALF : (k + 1) * HALF], raw.at[slot, level],
                    raw_send.at[0], raw_recv.at[level], (z, x, wrap(y + dy, NY), k),
                )
        remote(
            weights[level].at[:, :, theirs], raw.at[slot, level],
            raw_send.at[0], raw_recv.at[level], partner,
        )

    first = strip == 0
    last = strip == STRIPS - 1
    up5, up4 = repeat_matrix(32), repeat_matrix(64)

    def rows5(image, row, source, hidden=None):
        value = source.astype(F32)
        if hidden is not None:
            value = jnp.where(hidden, 0.0, value)
        put(x5, image, row, value)

    def rows4(image, row, source, coarse, hidden=None):
        value = source.astype(F32) + jnp.dot(up5, coarse, preferred_element_type=F32)
        if hidden is not None:
            value = jnp.where(hidden, 0.0, value)
        put(x4, image, row, value)

    def rows3(image, row, source, hidden=None):
        middle = x4[1, image, (row + 1) // 2]
        value = source.astype(F32) + jnp.dot(up4, middle, preferred_element_type=F32)
        if hidden is not None:
            value = jnp.where(hidden, 0.0, value)
        put(x3, image, row, value)

    for copy in loads:
        copy.wait()

    def own(image, _):
        rows5(image, 1, l5[image, 0])
        for q in (1, 2):
            rows4(image, q, l4[image, q - 1], l5[image, 0])
        for r in (1, 2, 3, 4):
            rows3(image, r, l3[image, r - 1])
        return 0

    with jax.named_scope("s5_own"):
        lax.fori_loop(0, B, own, 0)

    DIRECT = [slice(0, n) for n in DIRECT_TAPS]
    SPLIT = [slice(n, 9) for n in DIRECT_TAPS]
    quarter = pl.ds(2 * y, 2)
    pltpu.make_async_copy(raw.at[0], raw.at[0], local_sem.at[3]).wait()

    for level in range(3):
        with jax.named_scope(f"s6_raw{level}"):
            all_of(raw.at[0:7, level], raw_send.at[0], raw_recv.at[level]).wait_recv()
        for kh in range(3):
            rows = [raw[s, level, kh].astype(F32) for s in range(8)]
            for kw in range(3):
                tile = jnp.concatenate([r[kw : kw + 1] for r in rows], axis=0)
                w_all[c, level, x, z, kh * 3 + kw] = tile.astype(BF16)
        for block, part in (((0, 1),), ((1, 1), (0, 0)), ((2, 1), (1, 0), (2, 0)))[level]:
            for d in (4, 3, 5, 2, 6, 1, 7):
                ref = w_all.at[c, block, x, z, (SPLIT if part else DIRECT)[block]]
                remote(ref, ref, z_send.at[0], z_recv.at[block, part], z_ids[d - 1])

    for level, lateral, held, lowest in ((2, lat5, h5, 0), (1, lat4, h4, 1), (0, lat3, h3, 3)):
        remote(lateral.at[:, lowest], held.at[0], halo_send.at[level], halo_recv.at[level], next_id)
        remote(lateral.at[:, 0], held.at[1], halo_send.at[level], halo_recv.at[level], prev_id)

    def outer(image, _):
        rows5(image, 0, h5[0, image], first)
        rows5(image, 2, h5[1, image], last)
        rows4(image, 0, h4[0, image], h5[0, image], first)
        rows4(image, 3, h4[1, image], h5[1, image], last)
        rows3(image, 0, h3[0, image], first)
        rows3(image, 5, h3[1, image], last)
        return 0

    def to_partner(level, part, ref):
        remote(ref, ref, c_send.at[0], c_recv.at[level, part], partner)

    def after_z(level, part):
        taps = (SPLIT if part else DIRECT)[level]
        with jax.named_scope(f"z{level}{part}"):
            all_of(w_all.at[c, level, x, 0:7, taps], z_send.at[0], z_recv.at[level, part]).wait_recv()
        ref = w_all.at[c, level, x, quarter, taps] if part else w_all.at[c, level, x, :, taps]
        for d in (2, 1, 3):
            remote(ref, ref, x_send.at[part], x_recv.at[level, part], x_ids[d - 1])
        to_partner(level, part, w_all.at[c, level, x, :, taps])

    def after_x(level, part):
        with jax.named_scope(f"x{level}{part}"):
            if part:
                total = w_all.at[c, level, 0:3, 0:2, SPLIT[level]]
            else:
                total = w_all.at[c, level, 0:3, :, DIRECT[level]]
            all_of(total, x_send.at[part], x_recv.at[level, part]).wait_recv()
        for d in (1, 3, 2):
            where = wrap(x - d, NX)
            if part:
                ref = w_all.at[c, level, where, quarter, SPLIT[level]]
                for e in (2, 1, 3):
                    remote(ref, ref, y_send.at[0], y_recv.at[level], y_ids[e - 1])
            else:
                to_partner(level, part, w_all.at[c, level, where, :, DIRECT[level]])

    def after_y(level):
        with jax.named_scope(f"y{level}"):
            all_of(w_all.at[c, level, 0:3, 0:6, SPLIT[level]], y_send.at[0], y_recv.at[level]).wait_recv()
        for d in (1, 2, 3):
            to_partner(level, 1, w_all.at[c, level, wrap(x - d, NX), :, SPLIT[level]])

    def receive_partner(level, part):
        taps = (SPLIT if part else DIRECT)[level]
        with jax.named_scope(f"c{level}{part}"):
            all_of(w_all.at[other, level, :, :, taps], c_send.at[0], c_recv.at[level, part]).wait_recv()

    def ready(level, part):
        for t in range(9)[(SPLIT if part else DIRECT)[level]]:
            for half in range(2):
                for o in range(0, 32, 2):
                    pair = [
                        w_all[half, level, (o + k) % 4, (o + k) // 4, t].astype(F32) for k in range(2)
                    ]
                    w_tap[t, o * 8 : o * 8 + 16, half * HALF : (half + 1) * HALF] = jnp.concatenate(
                        pair, axis=0
                    ).astype(BF16)

    def products(pick, level, part):
        total = None
        for t in range(9)[(SPLIT if part else DIRECT)[level]]:
            term = lax.dot_general(
                pick(t // 3, t % 3), w_tap[t], (((1,), (1,)), ((), ())), preferred_element_type=F32
            )
            total = term if total is None else total + term
        return total

    def moments(level, image, parts):
        sums[2 * level, image : image + 1] = sum(jnp.sum(p, axis=0, keepdims=True) for p in parts)
        sums[2 * level + 1, image : image + 1] = sum(
            jnp.sum(p * p, axis=0, keepdims=True) for p in parts
        )

    def convolve(level, part, images, source, target, step):
        rows, width = LEVELS[level]
        for image in images:
            parts = []
            for top in range(0, rows, step):
                total = products(
                    lambda kh, kw: source[kw, image, top + kh : top + kh + step].reshape(step * width, C),
                    level, part,
                )
                if part:
                    total = target[image, top : top + step].reshape(step * width, C) + total
                    parts.append(total)
                target[image, top : top + step] = total.reshape(step, width, C)
            if part:
                moments(level, image, parts)

    def conv3(part, images):
        convolve(0, part, images, x3, f3, 2)

    def conv_small(level, part, source, target):
        rows, width = LEVELS[level]
        ready(level, part)
        block = B * width * rows
        total = products(
            lambda kh, kw: source[kw, :, kh : kh + rows].reshape(block, C), level, part
        )
        if part:
            total = target[...].reshape(block, C) + total
            for image in range(B):
                moments(level, image, [total[image * rows * width : (image + 1) * rows * width]])
        target[...] = total.reshape(B, rows, width, C)

    after_z(0, 1)
    after_z(1, 1)
    after_z(0, 0)
    after_x(0, 1)
    with jax.named_scope("s7_halo"):
        for level, held in ((2, h5), (1, h4), (0, h3)):
            all_of(held, halo_send.at[level], halo_recv.at[level]).wait_recv()
    lax.fori_loop(0, 2, outer, 0)
    after_z(2, 1)
    after_x(1, 1)
    lax.fori_loop(2, B, outer, 0)
    after_z(1, 0)
    after_z(2, 0)
    after_x(0, 0)
    after_x(2, 1)
    receive_partner(0, 0)
    with jax.named_scope("conv3Aa"):
        ready(0, 0)
        conv3(0, (0, 1))
    after_y(0)
    with jax.named_scope("conv3Ab"):
        conv3(0, (2, 3))
    after_x(1, 0)
    receive_partner(0, 1)
    with jax.named_scope("conv3Ca"):
        ready(0, 1)
        conv3(1, (0, 1))
    after_y(1)
    with jax.named_scope("conv3Cb"):
        conv3(1, (2, 3))
    after_x(2, 0)
    receive_partner(1, 0)
    with jax.named_scope("conv4A"):
        conv_small(1, 0, x4, f4)
    after_y(2)
    receive_partner(1, 1)
    with jax.named_scope("conv4C"):
        conv_small(1, 1, x4, f4)
    for part in (0, 1):
        receive_partner(2, part)
        with jax.named_scope(f"conv5{part}"):
            conv_small(2, part, x5, f5)

    def terms(value):
        high = value.astype(BF16)
        rest = value - high.astype(F32)
        middle = rest.astype(BF16)
        low = (rest - middle.astype(F32)).astype(BF16)
        return jnp.concatenate([high.astype(F32), middle.astype(F32), low.astype(F32)], axis=0).astype(BF16)

    channel = lax.broadcasted_iota(jnp.int32, (C, 128), 0)
    lane = lax.broadcasted_iota(jnp.int32, (C, 128), 1)
    member = (jnp.bitwise_and(lane, 31) == lax.shift_right_logical(channel, 3)).astype(F32).astype(BF16)
    owner = lax.shift_right_logical(lax.broadcasted_iota(jnp.int32, (8, 128), 1), 5)

    flat = jnp.concatenate([sums[:, image] for image in range(B)], axis=0)
    grouped = jnp.dot(terms(flat), member, preferred_element_type=F32)
    grouped = grouped[0:32] + grouped[32:64] + grouped[64:96]
    packed = jnp.zeros((8, 128), F32)
    for image in range(B):
        packed = jnp.where(owner == image, grouped[8 * image : 8 * image + 8], packed)
    stats[strip] = packed
    for who in plane_ids:
        remote(stats.at[strip], stats.at[strip], stat_send.at[0], stat_recv.at[0], who)
    with jax.named_scope("u1_stat"):
        all_of(stats.at[0 : STRIPS - 1], stat_send.at[0], stat_recv.at[0]).wait_recv()
    whole = jnp.sum(stats[...], axis=0)

    with jax.named_scope("v1_table"):
        pltpu.make_async_copy(params, params, local_sem.at[4]).wait()
        spreads = []
        for level, (rows, width) in enumerate(LEVELS):
            volume = float(rows * STRIPS * width * (C // G))
            mean = whole[2 * level : 2 * level + 1] / volume
            square = whole[2 * level + 1 : 2 * level + 2] / volume
            spread = jnp.maximum(square - mean * mean, 0.0)
            spreads += [mean, lax.rsqrt(spread + epsilon)]
        spreads += [jnp.zeros((2, 128), F32)]
        table = jnp.concatenate(spreads, axis=0)
        chosen = jnp.concatenate(
            [jnp.where(owner == image, table, 0.0) for image in range(B)], axis=0
        )
        wide = lax.dot_general(
            terms(chosen), member, (((1,), (1,)), ((), ())), preferred_element_type=F32
        )
        wide = wide[0:32] + wide[32:64] + wide[64:96]
        for image in range(B):
            spread_out = wide[8 * image : 8 * image + 8]
            for level in range(3):
                table_ref[level, 0, image : image + 1] = spread_out[2 * level : 2 * level + 1]
                table_ref[level, 1, image : image + 1] = (
                    spread_out[2 * level + 1 : 2 * level + 2] * params[2 * level]
                )
                table_ref[level, 2, image : image + 1] = params[2 * level + 1]

    with jax.named_scope("v2_sends"):
        all_of(raw.at[0:7], raw_send.at[0], raw_recv.at[0]).wait_send()
        for level, held in ((2, h5), (1, h4), (0, h3)):
            all_of(held, halo_send.at[level], halo_recv.at[level]).wait_send()
        all_of(w_all.at[c, :, 0, 0:7], z_send.at[0], z_recv.at[0, 0]).wait_send()
        for level in range(3):
            direct, split = DIRECT[level], SPLIT[level]
            all_of(w_all.at[c, level, 0:3, :, direct], x_send.at[0], x_recv.at[0, 0]).wait_send()
            all_of(w_all.at[c, level, 0:3, 0:2, split], x_send.at[1], x_recv.at[0, 1]).wait_send()
            all_of(w_all.at[c, level, 0:3, 0:6, split], y_send.at[0], y_recv.at[0]).wait_send()
        all_of(w_all.at[c], c_send.at[0], c_recv.at[0, 0]).wait_send()
        all_of(stats.at[0 : STRIPS - 1], stat_send.at[0], stat_recv.at[0]).wait_send()


def finish(f3, f4, f5, table, o3, o4, o5, s3, s4, s5, sem):
    copies = []
    for level, (source, held, target) in enumerate(((f3, s3, o3), (f4, s4, o4), (f5, s5, o5))):
        for image in range(B):
            center = table[level, 0, image : image + 1][None]
            scale = table[level, 1, image : image + 1][None]
            shift = table[level, 2, image : image + 1][None]
            held[image] = (source[image] - center) * scale + shift
            copy = pltpu.make_async_copy(held.at[image], target.at[image], sem.at[level, image])
            copy.start()
            copies.append(copy)
    for copy in copies:
        copy.wait()


def local(
    lateral3, lateral4, lateral5, conv_weight3, conv_weight4, conv_weight5,
    norm_gain3, norm_shift3, norm_gain4, norm_shift4, norm_gain5, norm_shift5,
):
    dma = pltpu.SemaphoreType.DMA
    vmem = pl.BlockSpec(memory_space=pltpu.VMEM)
    hbm = pl.BlockSpec(memory_space=pltpu.HBM)
    shapes = [jax.ShapeDtypeStruct((B, r, w, C), F32) for r, w in LEVELS]
    operands = [lateral3, lateral4, lateral5]
    operands += [w.reshape(3, 3, C) for w in (conv_weight3, conv_weight4, conv_weight5)]
    operands += [
        v.reshape(1, C)
        for v in (norm_gain3, norm_shift3, norm_gain4, norm_shift4, norm_gain5, norm_shift5)
    ]
    filtered = pl.pallas_call(
        kernel,
        out_shape=shapes + [jax.ShapeDtypeStruct((3, 3, B, C), F32)],
        in_specs=[hbm] * 12,
        out_specs=[vmem] * 4,
        scratch_shapes=[
            pltpu.VMEM((2, 3, NX, NZ, 9, 8, HALF), BF16),
            pltpu.VMEM((9, C, C), BF16),
            pltpu.VMEM((8, 3, 3, 3, HALF), BF16),
            pltpu.VMEM((B, 4, 128, C), BF16),
            pltpu.VMEM((B, 2, 64, C), BF16),
            pltpu.VMEM((B, 1, 32, C), BF16),
            pltpu.VMEM((2, B, 128, C), BF16),
            pltpu.VMEM((2, B, 64, C), BF16),
            pltpu.VMEM((2, B, 32, C), BF16),
            pltpu.VMEM((3, B, 6, 128, C), BF16),
            pltpu.VMEM((3, B, 4, 64, C), BF16),
            pltpu.VMEM((3, B, 3, 32, C), BF16),
            pltpu.VMEM((8, B, C), F32),
            pltpu.VMEM((STRIPS, 8, 128), F32),
            pltpu.VMEM((6, 1, C), F32),
            dma((5,)),
            dma((1,)), dma((3,)),
            dma((1,)), dma((3, 2)),
            dma((2,)), dma((3, 2)),
            dma((1,)), dma((3,)),
            dma((1,)), dma((3, 2)),
            dma((3,)), dma((3,)),
            dma((1,)), dma((1,)),
        ],
        compiler_params=pltpu.CompilerParams(
            collective_id=0, has_side_effects=True, vmem_limit_bytes=40 * 2**20
        ),
        name="neck",
    )(*(pltpu.with_memory_space_constraint(a, pltpu.HBM) for a in operands))

    return tuple(
        pl.pallas_call(
            finish,
            out_shape=shapes,
            in_specs=[vmem] * 4,
            out_specs=[hbm] * 3,
            scratch_shapes=[pltpu.VMEM(s.shape, F32) for s in shapes] + [dma((3, B))],
            compiler_params=pltpu.CompilerParams(vmem_limit_bytes=16 * 2**20),
            name="finish",
        )(*filtered)
    )


def solution(mesh):
    torus = Mesh(mesh.devices.reshape(NZ, NX, NY, NC), AXES)
    strips = P("z", SPACE, None, None)
    kernels = P(None, None, None, AXES)
    return jax.shard_map(
        local,
        mesh=torus,
        in_specs=(strips,) * 3 + (kernels,) * 3 + (P(),) * 6,
        out_specs=(strips,) * 3,
        check_vma=False,
    )
```

```python
import jax
import jax.numpy as jnp
from jax import lax
from jax.experimental import pallas as pl
from jax.experimental.pallas import tpu as pltpu
from jax.sharding import Mesh
from jax.sharding import PartitionSpec as P

SPACE = ("x", "y", "c")
AXES = ("z", "x", "y", "c")
MESH = pl.DeviceIdType.MESH
NZ, NX, NY, NC = 8, 4, 4, 2
STRIPS = NX * NY * NC
C, G, B = 256, 32, 4
HALF = 128
LEVELS = ((4, 128), (2, 64), (1, 32))
DIRECT_TAPS = (3, 3, 3)
epsilon = 1e-05
F32, BF16 = jnp.float32, jnp.bfloat16


def wrap(value, size):
    return lax.rem(value + 2 * size, size)


def put(ref, image, row, value):
    n = value.shape[0]
    rounded = value.astype(BF16)
    wide = rounded.astype(F32)
    place = lax.broadcasted_iota(jnp.int32, wide.shape, 0)
    ref[1, image, row] = rounded
    ref[0, image, row] = jnp.where(place == 0, 0.0, pltpu.roll(wide, 1, 0)).astype(BF16)
    ref[2, image, row] = jnp.where(place == n - 1, 0.0, pltpu.roll(wide, n - 1, 0)).astype(BF16)


def repeat_matrix(n):
    rows = lax.broadcasted_iota(jnp.int32, (2 * n, n), 0)
    columns = lax.broadcasted_iota(jnp.int32, (2 * n, n), 1)
    return (lax.shift_right_logical(rows, 1) == columns).astype(F32).astype(BF16)


def kernel(
    lat3, lat4, lat5, w3, w4, w5, g3, b3, g4, b4, g5, b5,
    f3, f4, f5, table_ref,
    w_all, w_tap, raw, l3, l4, l5, h3, h4, h5, x3, x4, x5, sums, stats, params,
    local_sem, raw_send, raw_recv, z_send, z_recv, x_send, x_recv, y_send, y_recv, c_send, c_recv,
    halo_send, halo_recv, stat_send, stat_recv,
):
    z, x, y, c = (lax.axis_index(a) for a in AXES)
    slot = y * 2 + c
    other = 1 - c
    strip = (x * NY + y) * 2 + c
    nxt, prv = wrap(strip + 1, STRIPS), wrap(strip - 1, STRIPS)
    next_id = (z, nxt // 8, lax.rem(nxt // 2, 4), lax.rem(nxt, 2))
    prev_id = (z, prv // 8, lax.rem(prv // 2, 4), lax.rem(prv, 2))
    partner = (z, x, y, other)

    ring_ids = [(z, x, wrap(y + dy, NY), k) for dy in (1, 2, 3) for k in range(2)] + [partner]
    y_ids = [(z, x, wrap(y + d, NY), c) for d in (1, 2, 3)]
    x_ids = [(z, wrap(x + d, NX), y, c) for d in (1, 2, 3)]
    z_ids = [(wrap(z + d, NZ), x, y, c) for d in range(1, NZ)]

    xs = [x] + [who[1] for who in x_ids]
    ys = [y] + [who[2] for who in y_ids]
    plane_ids = [
        (z, to_x, to_y, to_c)
        for i, j in sorted(
            ((i, j) for i in range(4) for j in range(4)),
            key=lambda p: abs(p[0] - 2) + abs(p[1] - 2),
        )
        for k in range(2)
        if i + j + k > 0
        for to_x, to_y, to_c in ((xs[i], ys[j], (c, other)[k]),)
    ]

    barrier = pltpu.get_barrier_semaphore()
    greeted = [z_ids[d - 1] for d in (4, 3, 5, 2, 6, 1, 7)] + x_ids + [next_id, prev_id] + ring_ids
    for who in greeted:
        pl.semaphore_signal(barrier, 1, device_id=who, device_id_type=MESH)

    loads = [
        pltpu.make_async_copy(lat5, l5, local_sem.at[0]),
        pltpu.make_async_copy(lat4, l4, local_sem.at[1]),
        pltpu.make_async_copy(lat3, l3, local_sem.at[2]),
    ]
    for copy in loads:
        copy.start()
    weights = (w3, w4, w5)
    mine = pl.ds(pl.multiple_of(c * HALF, HALF), HALF)
    theirs = pl.ds(pl.multiple_of(other * HALF, HALF), HALF)
    for level in range(3):
        pltpu.make_async_copy(
            weights[level].at[:, :, mine], raw.at[slot, level], local_sem.at[3]
        ).start()
    for i, source in enumerate((g3, b3, g4, b4, g5, b5)):
        pltpu.make_async_copy(source, params.at[i], local_sem.at[4]).start()

    def remote(source, target, sends, recvs, who):
        pltpu.make_async_remote_copy(
            source, target, sends, recvs, device_id=who, device_id_type=MESH
        ).start()

    def all_of(total, sends, recvs):
        return pltpu.make_async_remote_copy(
            total, total, sends, recvs, device_id=partner, device_id_type=MESH
        )

    with jax.named_scope("s3_barrier"):
        pl.semaphore_wait(barrier, len(greeted))

    for level in range(3):
        for dy in (2, 1, 3):
            for k in range(2):
                remote(
                    weights[level].at[:, :, k * HALF : (k + 1) * HALF], raw.at[slot, level],
                    raw_send.at[0], raw_recv.at[level], (z, x, wrap(y + dy, NY), k),
                )
        remote(
            weights[level].at[:, :, theirs], raw.at[slot, level],
            raw_send.at[0], raw_recv.at[level], partner,
        )

    first = strip == 0
    last = strip == STRIPS - 1
    up5, up4 = repeat_matrix(32), repeat_matrix(64)

    def rows5(image, row, source, hidden=None):
        value = source.astype(F32)
        if hidden is not None:
            value = jnp.where(hidden, 0.0, value)
        put(x5, image, row, value)

    def rows4(image, row, source, coarse, hidden=None):
        value = source.astype(F32) + jnp.dot(up5, coarse, preferred_element_type=F32)
        if hidden is not None:
            value = jnp.where(hidden, 0.0, value)
        put(x4, image, row, value)

    def rows3(image, row, source, hidden=None):
        middle = x4[1, image, (row + 1) // 2]
        value = source.astype(F32) + jnp.dot(up4, middle, preferred_element_type=F32)
        if hidden is not None:
            value = jnp.where(hidden, 0.0, value)
        put(x3, image, row, value)

    for copy in loads:
        copy.wait()

    def own(image, _):
        rows5(image, 1, l5[image, 0])
        for q in (1, 2):
            rows4(image, q, l4[image, q - 1], l5[image, 0])
        for r in (1, 2, 3, 4):
            rows3(image, r, l3[image, r - 1])
        return 0

    with jax.named_scope("s5_own"):
        lax.fori_loop(0, B, own, 0)

    DIRECT = [slice(0, n) for n in DIRECT_TAPS]
    SPLIT = [slice(n, 9) for n in DIRECT_TAPS]
    quarter = pl.ds(2 * y, 2)
    pltpu.make_async_copy(raw.at[0], raw.at[0], local_sem.at[3]).wait()

    for level in range(3):
        with jax.named_scope(f"s6_raw{level}"):
            all_of(raw.at[0:7, level], raw_send.at[0], raw_recv.at[level]).wait_recv()
        for kh in range(3):
            rows = [raw[s, level, kh].astype(F32) for s in range(8)]
            for kw in range(3):
                tile = jnp.concatenate([r[kw : kw + 1] for r in rows], axis=0)
                w_all[c, level, x, z, kh * 3 + kw] = tile.astype(BF16)
        for block, part in (((0, 1),), ((1, 1), (0, 0)), ((2, 1), (1, 0), (2, 0)))[level]:
            for d in (4, 3, 5, 2, 6, 1, 7):
                ref = w_all.at[c, block, x, z, (SPLIT if part else DIRECT)[block]]
                remote(ref, ref, z_send.at[0], z_recv.at[block, part], z_ids[d - 1])

    for level, lateral, held, lowest in ((2, lat5, h5, 0), (1, lat4, h4, 1), (0, lat3, h3, 3)):
        remote(lateral.at[:, lowest], held.at[0], halo_send.at[level], halo_recv.at[level], next_id)
        remote(lateral.at[:, 0], held.at[1], halo_send.at[level], halo_recv.at[level], prev_id)

    def outer(image, _):
        rows5(image, 0, h5[0, image], first)
        rows5(image, 2, h5[1, image], last)
        rows4(image, 0, h4[0, image], h5[0, image], first)
        rows4(image, 3, h4[1, image], h5[1, image], last)
        rows3(image, 0, h3[0, image], first)
        rows3(image, 5, h3[1, image], last)
        return 0

    def to_partner(level, part, ref):
        remote(ref, ref, c_send.at[0], c_recv.at[level, part], partner)

    def after_z(level, part):
        taps = (SPLIT if part else DIRECT)[level]
        with jax.named_scope(f"z{level}{part}"):
            all_of(w_all.at[c, level, x, 0:7, taps], z_send.at[0], z_recv.at[level, part]).wait_recv()
        ref = w_all.at[c, level, x, quarter, taps] if part else w_all.at[c, level, x, :, taps]
        for d in (2, 1, 3):
            remote(ref, ref, x_send.at[part], x_recv.at[level, part], x_ids[d - 1])
        to_partner(level, part, w_all.at[c, level, x, :, taps])

    def after_x(level, part):
        with jax.named_scope(f"x{level}{part}"):
            if part:
                total = w_all.at[c, level, 0:3, 0:2, SPLIT[level]]
            else:
                total = w_all.at[c, level, 0:3, :, DIRECT[level]]
            all_of(total, x_send.at[part], x_recv.at[level, part]).wait_recv()
        for d in (1, 3, 2):
            where = wrap(x - d, NX)
            if part:
                ref = w_all.at[c, level, where, quarter, SPLIT[level]]
                for e in (2, 1, 3):
                    remote(ref, ref, y_send.at[0], y_recv.at[level], y_ids[e - 1])
            else:
                to_partner(level, part, w_all.at[c, level, where, :, DIRECT[level]])

    def after_y(level):
        with jax.named_scope(f"y{level}"):
            all_of(w_all.at[c, level, 0:3, 0:6, SPLIT[level]], y_send.at[0], y_recv.at[level]).wait_recv()
        for d in (1, 2, 3):
            to_partner(level, 1, w_all.at[c, level, wrap(x - d, NX), :, SPLIT[level]])

    def receive_partner(level, part):
        taps = (SPLIT if part else DIRECT)[level]
        with jax.named_scope(f"c{level}{part}"):
            all_of(w_all.at[other, level, :, :, taps], c_send.at[0], c_recv.at[level, part]).wait_recv()

    def ready(level, part):
        for t in range(9)[(SPLIT if part else DIRECT)[level]]:
            for half in range(2):
                for o in range(0, 32, 2):
                    pair = [
                        w_all[half, level, (o + k) % 4, (o + k) // 4, t].astype(F32) for k in range(2)
                    ]
                    w_tap[t, o * 8 : o * 8 + 16, half * HALF : (half + 1) * HALF] = jnp.concatenate(
                        pair, axis=0
                    ).astype(BF16)

    def products(pick, level, part):
        total = None
        for t in range(9)[(SPLIT if part else DIRECT)[level]]:
            term = lax.dot_general(
                pick(t // 3, t % 3), w_tap[t], (((1,), (1,)), ((), ())), preferred_element_type=F32
            )
            total = term if total is None else total + term
        return total

    def moments(level, image, parts):
        sums[2 * level, image : image + 1] = sum(jnp.sum(p, axis=0, keepdims=True) for p in parts)
        sums[2 * level + 1, image : image + 1] = sum(
            jnp.sum(p * p, axis=0, keepdims=True) for p in parts
        )

    def convolve(level, part, images, source, target, step):
        rows, width = LEVELS[level]
        for image in images:
            parts = []
            for top in range(0, rows, step):
                total = products(
                    lambda kh, kw: source[kw, image, top + kh : top + kh + step].reshape(step * width, C),
                    level, part,
                )
                if part:
                    total = target[image, top : top + step].reshape(step * width, C) + total
                    parts.append(total)
                target[image, top : top + step] = total.reshape(step, width, C)
            if part:
                moments(level, image, parts)

    def conv3(part, images):
        convolve(0, part, images, x3, f3, 2)

    def conv_small(level, part, source, target):
        rows, width = LEVELS[level]
        ready(level, part)
        block = B * width * rows
        total = products(
            lambda kh, kw: source[kw, :, kh : kh + rows].reshape(block, C), level, part
        )
        if part:
            total = target[...].reshape(block, C) + total
            for image in range(B):
                moments(level, image, [total[image * rows * width : (image + 1) * rows * width]])
        target[...] = total.reshape(B, rows, width, C)

    after_z(0, 1)
    after_z(1, 1)
    after_z(0, 0)
    after_x(0, 1)
    with jax.named_scope("s7_halo"):
        for level, held in ((2, h5), (1, h4), (0, h3)):
            all_of(held, halo_send.at[level], halo_recv.at[level]).wait_recv()
    lax.fori_loop(0, 2, outer, 0)
    after_z(2, 1)
    after_x(1, 1)
    lax.fori_loop(2, B, outer, 0)
    after_z(1, 0)
    after_z(2, 0)
    after_x(0, 0)
    after_x(2, 1)
    receive_partner(0, 0)
    with jax.named_scope("conv3Aa"):
        ready(0, 0)
        conv3(0, (0, 1))
    after_y(0)
    with jax.named_scope("conv3Ab"):
        conv3(0, (2, 3))
    after_x(1, 0)
    receive_partner(0, 1)
    with jax.named_scope("conv3Ca"):
        ready(0, 1)
        conv3(1, (0, 1))
    after_y(1)
    with jax.named_scope("conv3Cb"):
        conv3(1, (2, 3))
    after_x(2, 0)
    receive_partner(1, 0)
    with jax.named_scope("conv4A"):
        conv_small(1, 0, x4, f4)
    after_y(2)
    receive_partner(1, 1)
    with jax.named_scope("conv4C"):
        conv_small(1, 1, x4, f4)
    for part in (0, 1):
        receive_partner(2, part)
        with jax.named_scope(f"conv5{part}"):
            conv_small(2, part, x5, f5)

    def terms(value):
        high = value.astype(BF16)
        rest = value - high.astype(F32)
        middle = rest.astype(BF16)
        low = (rest - middle.astype(F32)).astype(BF16)
        return jnp.concatenate([high.astype(F32), middle.astype(F32), low.astype(F32)], axis=0).astype(BF16)

    channel = lax.broadcasted_iota(jnp.int32, (C, 128), 0)
    lane = lax.broadcasted_iota(jnp.int32, (C, 128), 1)
    member = (jnp.bitwise_and(lane, 31) == lax.shift_right_logical(channel, 3)).astype(F32).astype(BF16)
    owner = lax.shift_right_logical(lax.broadcasted_iota(jnp.int32, (8, 128), 1), 5)

    flat = jnp.concatenate([sums[:, image] for image in range(B)], axis=0)
    grouped = jnp.dot(terms(flat), member, preferred_element_type=F32)
    grouped = grouped[0:32] + grouped[32:64] + grouped[64:96]
    packed = jnp.zeros((8, 128), F32)
    for image in range(B):
        packed = jnp.where(owner == image, grouped[8 * image : 8 * image + 8], packed)
    stats[strip] = packed
    for who in plane_ids:
        remote(stats.at[strip], stats.at[strip], stat_send.at[0], stat_recv.at[0], who)
    with jax.named_scope("u1_stat"):
        all_of(stats.at[0 : STRIPS - 1], stat_send.at[0], stat_recv.at[0]).wait_recv()
    whole = jnp.sum(stats[...], axis=0)

    with jax.named_scope("v1_table"):
        pltpu.make_async_copy(params, params, local_sem.at[4]).wait()
        spreads = []
        for level, (rows, width) in enumerate(LEVELS):
            volume = float(rows * STRIPS * width * (C // G))
            mean = whole[2 * level : 2 * level + 1] / volume
            square = whole[2 * level + 1 : 2 * level + 2] / volume
            spread = jnp.maximum(square - mean * mean, 0.0)
            spreads += [mean, lax.rsqrt(spread + epsilon)]
        spreads += [jnp.zeros((2, 128), F32)]
        table = jnp.concatenate(spreads, axis=0)
        chosen = jnp.concatenate(
            [jnp.where(owner == image, table, 0.0) for image in range(B)], axis=0
        )
        wide = lax.dot_general(
            terms(chosen), member, (((1,), (1,)), ((), ())), preferred_element_type=F32
        )
        wide = wide[0:32] + wide[32:64] + wide[64:96]
        for image in range(B):
            spread_out = wide[8 * image : 8 * image + 8]
            for level in range(3):
                table_ref[level, 0, image : image + 1] = spread_out[2 * level : 2 * level + 1]
                table_ref[level, 1, image : image + 1] = (
                    spread_out[2 * level + 1 : 2 * level + 2] * params[2 * level]
                )
                table_ref[level, 2, image : image + 1] = params[2 * level + 1]

    with jax.named_scope("v2_sends"):
        all_of(raw.at[0:7], raw_send.at[0], raw_recv.at[0]).wait_send()
        for level, held in ((2, h5), (1, h4), (0, h3)):
            all_of(held, halo_send.at[level], halo_recv.at[level]).wait_send()
        all_of(w_all.at[c, :, 0, 0:7], z_send.at[0], z_recv.at[0, 0]).wait_send()
        for level in range(3):
            direct, split = DIRECT[level], SPLIT[level]
            all_of(w_all.at[c, level, 0:3, :, direct], x_send.at[0], x_recv.at[0, 0]).wait_send()
            all_of(w_all.at[c, level, 0:3, 0:2, split], x_send.at[1], x_recv.at[0, 1]).wait_send()
            all_of(w_all.at[c, level, 0:3, 0:6, split], y_send.at[0], y_recv.at[0]).wait_send()
        all_of(w_all.at[c], c_send.at[0], c_recv.at[0, 0]).wait_send()
        all_of(stats.at[0 : STRIPS - 1], stat_send.at[0], stat_recv.at[0]).wait_send()


def finish(f3, f4, f5, table, o3, o4, o5, s3, s4, s5, sem):
    copies = []
    for level, (source, held, target) in enumerate(((f3, s3, o3), (f4, s4, o4), (f5, s5, o5))):
        for image in range(B):
            center = table[level, 0, image : image + 1][None]
            scale = table[level, 1, image : image + 1][None]
            shift = table[level, 2, image : image + 1][None]
            held[image] = (source[image] - center) * scale + shift
            copy = pltpu.make_async_copy(held.at[image], target.at[image], sem.at[level, image])
            copy.start()
            copies.append(copy)
    for copy in copies:
        copy.wait()


def local(
    lateral3, lateral4, lateral5, conv_weight3, conv_weight4, conv_weight5,
    norm_gain3, norm_shift3, norm_gain4, norm_shift4, norm_gain5, norm_shift5,
):
    dma = pltpu.SemaphoreType.DMA
    vmem = pl.BlockSpec(memory_space=pltpu.VMEM)
    hbm = pl.BlockSpec(memory_space=pltpu.HBM)
    shapes = [jax.ShapeDtypeStruct((B, r, w, C), F32) for r, w in LEVELS]
    operands = [lateral3, lateral4, lateral5]
    operands += [w.reshape(3, 3, C) for w in (conv_weight3, conv_weight4, conv_weight5)]
    operands += [
        v.reshape(1, C)
        for v in (norm_gain3, norm_shift3, norm_gain4, norm_shift4, norm_gain5, norm_shift5)
    ]
    filtered = pl.pallas_call(
        kernel,
        out_shape=shapes + [jax.ShapeDtypeStruct((3, 3, B, C), F32)],
        in_specs=[hbm] * 12,
        out_specs=[vmem] * 4,
        scratch_shapes=[
            pltpu.VMEM((2, 3, NX, NZ, 9, 8, HALF), BF16),
            pltpu.VMEM((9, C, C), BF16),
            pltpu.VMEM((8, 3, 3, 3, HALF), BF16),
            pltpu.VMEM((B, 4, 128, C), BF16),
            pltpu.VMEM((B, 2, 64, C), BF16),
            pltpu.VMEM((B, 1, 32, C), BF16),
            pltpu.VMEM((2, B, 128, C), BF16),
            pltpu.VMEM((2, B, 64, C), BF16),
            pltpu.VMEM((2, B, 32, C), BF16),
            pltpu.VMEM((3, B, 6, 128, C), BF16),
            pltpu.VMEM((3, B, 4, 64, C), BF16),
            pltpu.VMEM((3, B, 3, 32, C), BF16),
            pltpu.VMEM((8, B, C), F32),
            pltpu.VMEM((STRIPS, 8, 128), F32),
            pltpu.VMEM((6, 1, C), F32),
            dma((5,)),
            dma((1,)), dma((3,)),
            dma((1,)), dma((3, 2)),
            dma((2,)), dma((3, 2)),
            dma((1,)), dma((3,)),
            dma((1,)), dma((3, 2)),
            dma((3,)), dma((3,)),
            dma((1,)), dma((1,)),
        ],
        compiler_params=pltpu.CompilerParams(
            collective_id=0, has_side_effects=True, vmem_limit_bytes=40 * 2**20
        ),
        name="neck",
    )(*(pltpu.with_memory_space_constraint(a, pltpu.HBM) for a in operands))

    return tuple(
        pl.pallas_call(
            finish,
            out_shape=shapes,
            in_specs=[vmem] * 4,
            out_specs=[hbm] * 3,
            scratch_shapes=[pltpu.VMEM(s.shape, F32) for s in shapes] + [dma((3, B))],
            compiler_params=pltpu.CompilerParams(vmem_limit_bytes=16 * 2**20),
            name="finish",
        )(*filtered)
    )


def solution(mesh):
    torus = Mesh(mesh.devices.reshape(NZ, NX, NY, NC), AXES)
    strips = P("z", SPACE, None, None)
    kernels = P(None, None, None, AXES)
    return jax.shard_map(
        local,
        mesh=torus,
        in_specs=(strips,) * 3 + (kernels,) * 3 + (P(),) * 6,
        out_specs=(strips,) * 3,
        check_vma=False,
    )
```
